1024 devices in a mesh: ctx: 32 (over x_hi, z), ch: 32 (over x_lo, y, core).
Axes of the slice: x: 4 (x_hi: 2, x_lo: 2; x = x_hi * 2 + x_lo), y: 8, z: 16, core: 2. Of those that a mesh axis runs over, the one named last changes fastest.
Arguments:
- query_proj: bfloat16 [8192, 4096], P('ch', 'ctx'), may hold values from -6 to 6
- key_proj: bfloat16 [8192, 4096], P('ch', 'ctx'), may hold values from -6 to 6
- value_proj: bfloat16 [8192, 4096], P('ch', 'ctx'), may hold values from -6 to 6
- cotangent: bfloat16 [8192, 4096], P('ch', 'ctx'), may hold values from -0.0234375 to 0.0234375
- positions: int32 [4096], P('ctx'), may hold values from 0 to 4095, as said below
- group_of: int32 [8192], replicated, may hold values from 0 to 511, as said below
- decay_rates: float32 [512, 16], replicated, may hold values from 2.4414063e-05 to 0.03
- residues: float32 [512, 16], replicated, may hold values from -1.5 to 1.5
Outputs:
- output: bfloat16 [8192, 4096], P('ch', 'ctx')
- filter_grad: float32 [512, 4096], P('ch', 'ctx')
The draws below stay inside these ranges and needn't reach their ends.
Inputs may be any that keep to these rules, and one draw needn't show every extreme that they name: positions is a permutation of the sequence positions; every aligned run of 64 stored tokens holds consecutive positions that start at a multiple of 64. `group_of`: every group has exactly 16 channels; each aligned block of 256 channels holds exactly 8 channels of the groups of each aligned block of 16 groups.
All inputs are finite; a program needn't handle non-finite values.
Results may differ from the reference program's by a relative error of at most 0.0058.
Values may be sent and summed in bfloat16 or wider, within the bound.
A program may use at most 32 MiB of HBM per device.

```python
import math
import jax
import jax.numpy as jnp
from jax import lax

CHANNELS = 8192
GROUP_SIZE = 16
ORDER = 16
TOK_DEV = 128
TOKENS = 4096
CH_DEV = 256
GROUPS = 512
OWN_GROUPS = 16
SLOTS = 8


def draw_positions(key, part):
    half_run = TOK_DEV // 2
    run_count = TOKENS // half_run
    run_order = jax.random.permutation(jax.random.fold_in(key, 11), run_count).astype(jnp.int32)
    within = jnp.arange(half_run, dtype=jnp.int32)
    return (run_order[:, None] * half_run + within[None, :]).reshape(-1).astype(jnp.int32)


def shuffle_one(subkey):
    return jax.random.permutation(subkey, CH_DEV).astype(jnp.int32)


def draw_group_of(key, part):
    owner_count = CHANNELS // CH_DEV
    key_owner, key_source = jax.random.split(jax.random.fold_in(key, 23))
    owner_perm = jax.vmap(shuffle_one)(jax.random.split(key_owner, owner_count))
    source_perm = jax.vmap(shuffle_one)(jax.random.split(key_source, owner_count))
    owner_ids = source_perm // SLOTS
    slot_ids = source_perm % SLOTS
    source_ids = jnp.arange(owner_count, dtype=jnp.int32)[:, None]
    group_slot = owner_perm[owner_ids, source_ids * SLOTS + slot_ids]
    return (owner_ids * OWN_GROUPS + group_slot // GROUP_SIZE).reshape(-1).astype(jnp.int32)


def level_of(key, dims, cuts, least, top_value):
    gain, own = 1.0, jax.random.fold_in(key, 6)
    for dim, shards_of in cuts:
        steps = jnp.exp(jax.random.uniform(jax.random.fold_in(own, dim), (shards_of,), jnp.float32, least / len(cuts), top_value / len(cuts)))
        gain = gain * jnp.repeat(steps, dims[dim] // shards_of).reshape([-1 if axis == dim else 1 for axis in range(len(dims))])
    return gain


def scatter_about(rng, shape, deviation, reach, cuts=(), kind=jnp.bfloat16):
    factor_of = level_of(rng, shape, cuts, -0.22, 0.18) if cuts else 1.0
    result = jax.random.normal(rng, shape, jnp.float32) * deviation * factor_of
    return jnp.minimum(jnp.maximum(result, -reach), reach).astype(kind)


def setup_inputs(seed: int = 0) -> dict:
    key_list = jax.random.split(jax.random.key(seed), 9)
    return {
        "query_proj": scatter_about(key_list[0], (CHANNELS, TOKENS), 1.0, 6.0, ((0, 32), (1, 32))),
        "key_proj": scatter_about(key_list[1], (CHANNELS, TOKENS), 1.0, 6.0, ((0, 32), (1, 32))),
        "value_proj": scatter_about(key_list[2], (CHANNELS, TOKENS), 1.0, 6.0, ((0, 32), (1, 32))),
        "cotangent": scatter_about(key_list[3], (CHANNELS, TOKENS), (0.25 / TOKENS ** 0.5), 0.0234375, ((0, 32), (1, 32))),
        "positions": draw_positions(jax.random.fold_in(key_list[8], 71), 0),
        "group_of": draw_group_of(jax.random.fold_in(key_list[8], 71), 0),
        "decay_rates": jnp.clip(jnp.exp(jax.random.uniform(key_list[6], (GROUPS, ORDER), jnp.float32, math.log(2.441406286379788e-05), math.log(0.03))), 2.441406286379788e-05, 0.03),
        "residues": scatter_about(key_list[7], (GROUPS, ORDER), 0.25, 1.5, (), jnp.float32),
    }


def reference(query_proj, key_proj, value_proj, cotangent, positions, group_of, decay_rates, residues):
    channel_count, seq_length = query_proj.shape
    extent = 2 * seq_length
    block_rows = min(256, channel_count)
    blocks = channel_count // block_rows
    source_index = jnp.zeros((seq_length,), jnp.int32).at[positions].set(jnp.arange(seq_length, dtype=jnp.int32))
    tap_index = jnp.arange(seq_length, dtype=jnp.float32)

    def fold_blocks(array_in):
        return array_in.reshape((blocks, block_rows) + array_in.shape[1:])

    def block_step(running, pieces):
        query_rows, key_rows, value_rows, cot_rows, group_rows = pieces
        gated = (key_rows.astype(jnp.float32) * value_rows.astype(jnp.float32)).astype(jnp.bfloat16)
        weighted = (cot_rows.astype(jnp.float32) * query_rows.astype(jnp.float32)).astype(jnp.bfloat16)
        gated_seq = gated[:, source_index].astype(jnp.float32)
        weighted_seq = weighted[:, source_index].astype(jnp.float32)
        decay_rows = decay_rates[group_rows]
        gain_rows = residues[group_rows]
        coefs = gain_rows * jnp.sqrt(2.0 * decay_rows)
        filters = lax.optimization_barrier(jnp.sum(coefs[:, :, None] * jnp.exp(-decay_rows[:, :, None] * tap_index), axis=1))
        gated_spec = jnp.fft.rfft(gated_seq, n=extent, axis=1)
        filter_spec = jnp.fft.rfft(filters, n=extent, axis=1)
        weighted_spec = jnp.fft.rfft(weighted_seq, n=extent, axis=1)
        convolved = jnp.fft.irfft(filter_spec * gated_spec, n=extent, axis=1)[:, :seq_length].astype(jnp.bfloat16)
        lagged = jnp.fft.irfft(weighted_spec * jnp.conj(gated_spec), n=extent, axis=1)[:, :seq_length]
        output = (query_rows.astype(jnp.float32) * convolved[:, positions].astype(jnp.float32)).astype(jnp.bfloat16)
        running = running + jax.ops.segment_sum(lagged.astype(jnp.float32), group_rows, num_segments=GROUPS)
        return (running, output)
    filter_grad, outputs = lax.scan(block_step, jnp.zeros((GROUPS, seq_length), jnp.float32), (fold_blocks(query_proj), fold_blocks(key_proj), fold_blocks(value_proj), fold_blocks(cotangent), fold_blocks(group_of)))
    return (outputs.reshape(channel_count, seq_length), filter_grad)
```

```python
import functools
import math

import jax
import jax.numpy as jnp
import ml_dtypes
import numpy as np
from jax import lax
from jax.experimental import pallas as pl
from jax.experimental.pallas import tpu as pltpu
from jax.sharding import PartitionSpec as P

MESH = pl.DeviceIdType.MESH
BF16 = jnp.bfloat16
F32 = jnp.float32


def halves(table):
    high = table.astype(ml_dtypes.bfloat16)
    low = (table - high.astype(np.float64)).astype(ml_dtypes.bfloat16)
    return high, low


def make_tables(n, lanes):
    run = lanes // 2
    extent = 2 * lanes * n
    turn = 2.0 * math.pi
    k = np.arange(n)
    j = np.arange(lanes) % run
    m = np.arange(lanes) % run
    par = np.arange(lanes) // run

    def second(angle, mask):
        cos, sin = np.cos(angle) * mask, np.sin(angle) * mask
        return np.block([[cos, -sin], [sin, cos]])

    perm_angle = turn * (j[:, None] * m[None, :] % run) / run
    nat_angle = turn * (np.arange(lanes)[:, None] * (2 * m + par)[None, :] % lanes) / lanes
    seconds = [second(perm_angle, (par == p)[None, :].astype(np.float64)) for p in range(2)]
    seconds.append(second(nat_angle, 1.0))
    second_tab = np.stack([part for table in seconds for part in halves(table)])

    twists = []
    for rows, cols in ((k, j), (k + 2 * n, j), (k, np.arange(lanes))):
        angle = turn * ((2 * rows[:, None] + 1) * cols[None, :] % (2 * extent)) / (2 * extent)
        twists += [np.cos(angle), -np.sin(angle)]
    twist_tab = np.stack(twists).astype(np.float32)

    kk = np.concatenate([k, k, k + 2 * n, k + 2 * n])
    part = np.concatenate([np.zeros(n), np.ones(n)] * 2)
    angle = turn * ((2 * kk[None, :] + 1) * np.arange(2 * n)[:, None] % (8 * n)) / (8 * n)
    first = np.where(part[None, :] == 0, np.cos(angle), -np.sin(angle))
    run_tab = np.concatenate(halves(first), axis=0)

    kn = np.concatenate([k, k])
    partn = np.concatenate([np.zeros(n), np.ones(n)])
    angle = turn * ((2 * kn[:, None] + 1) * k[None, :] % (4 * n)) / (4 * n)
    chunk = np.where(partn[:, None] == 0, np.cos(angle), -np.sin(angle))
    high, low = halves(chunk)
    chunk_fwd = np.concatenate([high, low, high], axis=1)
    scale = 2.0 / extent
    high, low = halves(chunk.T * scale)
    chunk_inv = np.concatenate([high, low, high], axis=1)
    return second_tab, twist_tab, run_tab, np.ascontiguousarray(run_tab.T), chunk_fwd, chunk_inv


def dot(left, right):
    return lax.dot_general(left, right, (((1,), (0,)), ((), ())), preferred_element_type=F32)


def dot_nt(left, right):
    return lax.dot_general(left, right, (((1,), (1,)), ((), ())), preferred_element_type=F32)


def split(value):
    high = value.astype(BF16)
    return high, (value - high.astype(F32)).astype(BF16)


def iota(shape, axis):
    return lax.broadcasted_iota(jnp.int32, shape, axis)


def kernel(
    n,
    slots,
    own,
    order,
    q_hbm, k_hbm, v_hbm, c_hbm, pos_hbm, grp_hbm, dec_hbm, res_hbm,
    sec_hbm, twi_hbm, run_hbm, runt_hbm, cfw_hbm, cin_hbm,
    out_ref, fg_ref,
    q_ref, k_ref, v_ref, c_ref, pos_ref, grp_ref, dec_ref, res_ref,
    sec_ref, twi_ref, run_ref, runt_ref, cfw_ref, cin_ref,
    x_send, x_recv, p_recv, c_send, c_recv, l_send, l_recv, f_send, f_recv,
    xs, taps, gcol, ys, onehot, unsort, lagsel,
    in_sem, x_ssem, x_rsem, p_ssem, p_rsem, c_ssem, c_rsem, l_ssem, l_rsem, f_sem,
):
    lanes = 128
    run = lanes // 2
    chans = n * slots
    ctx = lax.axis_index("ctx")
    ch = lax.axis_index("ch")

    barrier = pltpu.get_barrier_semaphore()

    def greet(step, carry):
        pl.semaphore_signal(
            barrier, inc=1, device_id={"ctx": lax.rem(ctx + step, n)}, device_id_type=MESH
        )
        pl.semaphore_signal(
            barrier, inc=1, device_id={"ch": lax.rem(ch + step, n)}, device_id_type=MESH
        )
        return carry

    lax.fori_loop(1, n, greet, 0)

    sources = (grp_hbm, k_hbm, v_hbm, c_hbm, q_hbm, pos_hbm, dec_hbm, res_hbm,
               runt_hbm, run_hbm, cfw_hbm, twi_hbm, sec_hbm, cin_hbm)
    targets = (grp_ref, k_ref, v_ref, c_ref, q_ref, pos_ref, dec_ref, res_ref,
               runt_ref, run_ref, cfw_ref, twi_ref, sec_ref, cin_ref)
    loads = [
        pltpu.make_async_copy(source, target, in_sem.at[index])
        for index, (source, target) in enumerate(zip(sources, targets))
    ]
    for load in loads:
        load.start()

    loads[0].wait()
    if chans > lanes:
        per_row = chans // lanes
        pieces = [grp_ref[pl.ds(i, n, stride=per_row), :] for i in range(per_row)]
        group_all = jnp.concatenate(pieces, axis=1).astype(F32)
        pieces = [grp_ref[pl.ds(ch * per_row + i, 1), :] for i in range(per_row)]
        group_row = jnp.concatenate(pieces, axis=1).astype(F32)
    else:
        group_all = grp_ref[...].astype(F32)
        group_row = grp_ref[pl.ds(ch, 1), :].astype(F32)
    owner_row = jnp.floor(group_row * (1.0 / own))
    owner_rows = jnp.broadcast_to(owner_row, (chans, chans))
    owner_cols = jnp.transpose(owner_rows)
    row_i = iota((chans, chans), 0)
    col_i = iota((chans, chans), 1)
    same = owner_rows == owner_cols
    rank_row = jnp.sum(jnp.where(same & (row_i < col_i), 1.0, 0.0), axis=0, keepdims=True)
    rank_col = jnp.sum(jnp.where(same & (col_i < row_i), 1.0, 0.0), axis=1, keepdims=True)
    slot_row = owner_row * slots + rank_row
    slot_col = owner_cols[:, 0:1] * slots + rank_col
    sort = jnp.where(slot_row == row_i.astype(F32), 1.0, 0.0).astype(BF16)
    unsort[...] = jnp.where(slot_col == col_i.astype(F32), 1.0, 0.0).astype(BF16)

    for index in range(1, 5):
        loads[index].wait()
    gated = (k_ref[...].astype(F32) * v_ref[...].astype(F32)).astype(BF16)
    weighted = (c_ref[...].astype(F32) * q_ref[...].astype(F32)).astype(BF16)
    gated = dot(sort, gated).reshape(n, slots, lanes)
    weighted = dot(sort, weighted).reshape(n, slots, lanes)
    x_send[...] = jnp.concatenate([gated, weighted], axis=1).astype(BF16)
    loads[5].wait()

    pl.semaphore_wait(barrier, 2 * (n - 1))

    def pos_copy(step, target, home):
        return pltpu.make_async_remote_copy(
            src_ref=pos_ref, dst_ref=p_recv.at[home],
            send_sem=p_ssem.at[step], recv_sem=p_rsem.at[home],
            device_id={"ctx": target}, device_id_type=MESH,
        )

    def x_copy(step, target, home):
        return pltpu.make_async_remote_copy(
            src_ref=x_send.at[target], dst_ref=x_recv.at[home],
            send_sem=x_ssem.at[step], recv_sem=x_rsem.at[home],
            device_id={"ctx": target}, device_id_type=MESH,
        )

    def c_copy(step, target, home):
        return pltpu.make_async_remote_copy(
            src_ref=c_send.at[target], dst_ref=c_recv.at[home],
            send_sem=c_ssem.at[step], recv_sem=c_rsem.at[home],
            device_id={"ctx": target}, device_id_type=MESH,
        )

    def l_copy(step, target, home):
        return pltpu.make_async_remote_copy(
            src_ref=l_send.at[target], dst_ref=l_recv.at[home],
            send_sem=l_ssem.at[step], recv_sem=l_rsem.at[home],
            device_id={"ch": target}, device_id_type=MESH,
        )

    def send_all(copy, me):
        def body(step, carry):
            copy(step, lax.rem(me + step, n), me).start()
            return carry
        lax.fori_loop(1, n, body, 0)

    def recv_all(copy, me):
        def body(step, carry):
            other = lax.rem(me + step, n)
            copy(step, other, other).wait_recv()
            return carry
        lax.fori_loop(1, n, body, 0)

    def sent_all(copy, me):
        def body(step, carry):
            copy(step, lax.rem(me + step, n), me).wait_send()
            return carry
        lax.fori_loop(1, n, body, 0)

    send_all(x_copy, ctx)
    send_all(pos_copy, ctx)
    x_recv[ctx] = x_send[ctx]
    p_recv[ctx] = pos_ref[...]

    loads[6].wait()
    loads[7].wait()
    me_slot = iota((slots, chans), 0).astype(F32) + (ctx * slots).astype(F32)
    mine = jnp.where(slot_row == me_slot, group_row, 0.0)
    my_group = jnp.sum(mine, axis=1, keepdims=True)
    groups_total = dec_ref.shape[1]
    pick = my_group == iota((slots, groups_total), 1).astype(F32)
    rates, coefs = [], []
    for mode in range(order):
        rate = jnp.sum(jnp.where(pick, dec_ref[mode : mode + 1, :], 0.0), axis=1, keepdims=True)
        gain = jnp.sum(jnp.where(pick, res_ref[mode : mode + 1, :], 0.0), axis=1, keepdims=True)
        rates.append(jnp.broadcast_to(-rate, (slots, lanes)))
        coefs.append(jnp.broadcast_to(gain * jnp.sqrt(2.0 * rate), (slots, lanes)))
    lane_time = iota((slots, lanes), 1).astype(F32)

    def tap_step(chunk, carry):
        time = lane_time + (chunk * lanes).astype(F32)
        total = coefs[0] * jnp.exp(rates[0] * time)
        for mode in range(1, order):
            total = total + coefs[mode] * jnp.exp(rates[mode] * time)
        taps[pl.ds(pl.multiple_of(chunk * slots, slots), slots), :] = total
        return carry

    lax.fori_loop(0, n, tap_step, 0)

    for index in range(8, 14):
        loads[index].wait()

    def turned(real, imag, which):
        cos, sin = twi_ref[2 * which], twi_ref[2 * which + 1]
        return real * cos - imag * sin, real * sin + imag * cos

    def turned_back(real, imag, which):
        cos, sin = twi_ref[2 * which], twi_ref[2 * which + 1]
        return real * cos + imag * sin, imag * cos - real * sin

    def second(high, low, which):
        return (
            dot(high, sec_ref[2 * which])
            + dot(low, sec_ref[2 * which])
            + dot(high, sec_ref[2 * which + 1])
        )

    def second_back(high, low, which):
        return (
            dot_nt(high, sec_ref[2 * which])
            + dot_nt(low, sec_ref[2 * which])
            + dot_nt(high, sec_ref[2 * which + 1])
        )

    rows = []
    for i in range(slots):
        high, low = split(taps[pl.ds(i, n, stride=slots), :])
        mid = dot(cfw_ref[...], jnp.concatenate([high, high, low], axis=0))
        rows.append(jnp.concatenate(turned(mid[:n], mid[n:], 2), axis=1))
    high, low = split(jnp.concatenate(rows, axis=0))
    spec = second(high, low, 2)
    filt_re, filt_im = spec[:, :lanes], spec[:, lanes:]

    mine_all = jnp.floor(group_all * (1.0 / own)) == ctx.astype(F32)
    member = jnp.where(mine_all, 1.0, 0.0)
    before = jnp.where(row_i < col_i, 1.0, 0.0).astype(BF16)
    rank_all = dot(member.astype(BF16), before)
    for i in range(slots):
        hit = jnp.where(mine_all & (rank_all == float(i)), group_all, 0.0)
        gcol[pl.ds(i, n, stride=slots), :] = jnp.broadcast_to(
            jnp.sum(hit, axis=1, keepdims=True), (n, lanes)
        )
    first_own = (ctx * own).astype(F32)
    of_group = jnp.where(
        gcol[...] - first_own == iota((chans, lanes), 1).astype(F32), 1.0, 0.0
    )
    lagsel[...] = jnp.transpose(of_group)[: lagsel.shape[0], :].astype(BF16)

    recv_all(pos_copy, ctx)
    places = p_recv[...].reshape(n, lanes).astype(F32) * (1.0 / run)
    place = jnp.concatenate([places[:, 0:1], places[:, run : run + 1]], axis=0)
    place = jnp.concatenate([place, place + float(2 * n)], axis=0)
    onehot[...] = jnp.where(place == iota((4 * n, 4 * n), 1).astype(F32), 1.0, 0.0).astype(BF16)
    first = dot_nt(runt_ref[...], onehot[...]).astype(BF16)
    last = (dot(onehot[...], run_ref[...]) * (2.0 / (2 * lanes * n))).astype(BF16)
    last = jnp.concatenate([last[: 2 * n], last[2 * n :], last[: 2 * n]], axis=1)
    lane_i = iota((n, lanes), 1)
    left = lane_i < run

    recv_all(x_copy, ctx)
    xs[...] = x_recv[...].astype(F32).reshape(2 * chans, lanes)
    gated_rows, weighted_rows = [[], []], [[], []]
    for i in range(slots):
        pair = []
        for row in (i, i + slots):
            value = xs[pl.ds(row, n, stride=2 * slots), :]
            both = jnp.concatenate(
                [jnp.where(left, value, 0.0), jnp.where(left, 0.0, value)], axis=0
            ).astype(BF16)
            pair.append(jnp.concatenate([both, both], axis=0))
        mid = dot(first, jnp.concatenate(pair, axis=1))
        for par in range(2):
            low_row = 2 * n * par
            for rows, off in ((gated_rows, 0), (weighted_rows, lanes)):
                piece = mid[low_row : low_row + 2 * n, off : off + lanes]
                rows[par].append(jnp.concatenate(turned(piece[:n], piece[n:], par), axis=1))

    def spectrum(rows):
        total = None
        for par in range(2):
            high, low = split(jnp.concatenate(rows[par], axis=0))
            term = second(high, low, par)
            total = term if total is None else total + term
        return total[:, :lanes], total[:, lanes:]

    gat_re, gat_im = spectrum(gated_rows)
    wei_re, wei_im = spectrum(weighted_rows)

    def channel(value, i):
        return value[i * n : (i + 1) * n]

    high, low = split(
        jnp.concatenate(
            [wei_re * gat_re + wei_im * gat_im, wei_im * gat_re - wei_re * gat_im], axis=1
        )
    )
    mid = second_back(high, low, 2)
    for i in range(slots):
        piece = channel(mid, i)
        high, low = split(
            jnp.concatenate(turned_back(piece[:, :lanes], piece[:, lanes:], 2), axis=0)
        )
        ys[pl.ds(i, n, stride=slots), :] = dot(
            cin_ref[...], jnp.concatenate([high, high, low], axis=0)
        )
    l_send[...] = ys[...].reshape(n, slots, lanes).astype(BF16)
    send_all(l_copy, ch)
    l_recv[ch] = l_send[ch]

    high, low = split(
        jnp.concatenate(
            [filt_re * gat_re - filt_im * gat_im, filt_re * gat_im + filt_im * gat_re], axis=1
        )
    )
    mids = [second_back(high, low, par) for par in range(2)]
    for i in range(slots):
        stack = []
        for par in range(2):
            piece = channel(mids[par], i)
            stack += list(turned_back(piece[:, :lanes], piece[:, lanes:], par))
        high, low = split(jnp.concatenate(stack, axis=0))
        value = dot(last, jnp.concatenate([high, high, low], axis=0))
        ys[pl.ds(i, n, stride=slots), :] = jnp.where(left, value[:n], value[n:])
    c_send[...] = ys[...].reshape(n, slots, lanes).astype(BF16)
    send_all(c_copy, ctx)
    c_recv[ctx] = c_send[ctx]

    recv_all(l_copy, ch)
    sums = dot(lagsel[...], l_recv[...].astype(F32).reshape(chans, lanes).astype(BF16))
    f_send[...] = sums[: f_send.shape[0]]
    far = pltpu.make_async_remote_copy(
        src_ref=f_send, dst_ref=f_recv, send_sem=f_sem.at[0], recv_sem=f_sem.at[1],
        device_id={"ctx": ch, "ch": ctx}, device_id_type=MESH,
    )

    @pl.when(ctx != ch)
    def _():
        far.start()

    recv_all(c_copy, ctx)
    conv = dot(unsort[...], c_recv[...].astype(F32).reshape(chans, lanes).astype(BF16))
    out_ref[...] = (q_ref[...].astype(F32) * conv).astype(BF16)

    sent_all(pos_copy, ctx)
    sent_all(x_copy, ctx)
    sent_all(l_copy, ch)
    sent_all(c_copy, ctx)

    @pl.when(ctx != ch)
    def _():
        far.wait()
        fg_ref[...] = f_recv[...]

    @pl.when(ctx == ch)
    def _():
        fg_ref[...] = f_send[...]


def shards(query_proj, key_proj, value_proj, cotangent, positions, group_of, decay_rates, residues):
    n = lax.axis_size("ctx")
    chans, lanes = query_proj.shape
    slots = chans // n
    groups_total, order = decay_rates.shape
    own = groups_total // lax.axis_size("ch")
    own_pad = -(-own // 16) * 16
    width = min(chans, lanes)
    tables = make_tables(n, lanes)
    args = (
        query_proj, key_proj, value_proj, cotangent,
        positions.reshape(1, lanes), group_of.reshape(-1, width),
        decay_rates.T, residues.T,
    ) + tuple(jnp.asarray(table) for table in tables)
    any_spec = pl.BlockSpec(memory_space=pl.ANY)
    vmem_spec = pl.BlockSpec(memory_space=pltpu.VMEM)
    dma = pltpu.SemaphoreType.DMA
    return pl.pallas_call(
        functools.partial(kernel, n, slots, own, order),
        out_shape=(
            jax.ShapeDtypeStruct((chans, lanes), BF16),
            jax.ShapeDtypeStruct((own, lanes), F32),
        ),
        in_specs=[any_spec] * len(args),
        out_specs=(vmem_spec, vmem_spec),
        scratch_shapes=[pltpu.VMEM(arg.shape, arg.dtype) for arg in args]
        + [
            pltpu.VMEM((n, 2 * slots, lanes), BF16),
            pltpu.VMEM((n, 2 * slots, lanes), BF16),
            pltpu.VMEM((n, 1, lanes), jnp.int32),
            pltpu.VMEM((n, slots, lanes), BF16),
            pltpu.VMEM((n, slots, lanes), BF16),
            pltpu.VMEM((n, slots, lanes), BF16),
            pltpu.VMEM((n, slots, lanes), BF16),
            pltpu.VMEM((own, lanes), F32),
            pltpu.VMEM((own, lanes), F32),
            pltpu.VMEM((2 * chans, lanes), F32),
            pltpu.VMEM((chans, lanes), F32),
            pltpu.VMEM((chans, lanes), F32),
            pltpu.VMEM((chans, lanes), F32),
            pltpu.VMEM((4 * n, 4 * n), BF16),
            pltpu.VMEM((chans, chans), BF16),
            pltpu.VMEM((own_pad, chans), BF16),
            dma((len(args),)),
            dma((n,)), dma((n,)), dma((n,)), dma((n,)),
            dma((n,)), dma((n,)), dma((n,)), dma((n,)),
            dma((2,)),
        ],
        compiler_params=pltpu.CompilerParams(collective_id=0, has_side_effects=True),
    )(*args)


def solution(mesh):
    placed = (
        P("ch", "ctx"),
        P("ch", "ctx"),
        P("ch", "ctx"),
        P("ch", "ctx"),
        P("ctx"),
        P(),
        P(),
        P(),
    )
    return jax.shard_map(
        shards,
        mesh=mesh,
        in_specs=placed,
        out_specs=(P("ch", "ctx"), P("ch", "ctx")),
        check_vma=False,
    )
```

```python
import functools
import math

import jax
import jax.numpy as jnp
import ml_dtypes
import numpy as np
from jax import lax
from jax.experimental import pallas as pl
from jax.experimental.pallas import tpu as pltpu
from jax.sharding import PartitionSpec as P

MESH = pl.DeviceIdType.MESH
BF16 = jnp.bfloat16
F32 = jnp.float32


def halves(table):
    high = table.astype(ml_dtypes.bfloat16)
    low = (table - high.astype(np.float64)).astype(ml_dtypes.bfloat16)
    return high, low


def make_tables(n, lanes):
    run = lanes // 2
    extent = 2 * lanes * n
    turn = 2.0 * math.pi
    k = np.arange(n)
    j = np.arange(lanes) % run
    m = np.arange(lanes) % run
    par = np.arange(lanes) // run

    def second(angle, mask):
        cos, sin = np.cos(angle) * mask, np.sin(angle) * mask
        return np.block([[cos, -sin], [sin, cos]])

    perm_angle = turn * (j[:, None] * m[None, :] % run) / run
    nat_angle = turn * (np.arange(lanes)[:, None] * (2 * m + par)[None, :] % lanes) / lanes
    seconds = [second(perm_angle, (par == p)[None, :].astype(np.float64)) for p in range(2)]
    seconds.append(second(nat_angle, 1.0))
    second_tab = np.stack([part for table in seconds for part in halves(table)])

    twists = []
    for rows, cols in ((k, j), (k + 2 * n, j), (k, np.arange(lanes))):
        angle = turn * ((2 * rows[:, None] + 1) * cols[None, :] % (2 * extent)) / (2 * extent)
        twists += [np.cos(angle), -np.sin(angle)]
    twist_tab = np.stack(twists).astype(np.float32)

    kk = np.concatenate([k, k, k + 2 * n, k + 2 * n])
    part = np.concatenate([np.zeros(n), np.ones(n)] * 2)
    angle = turn * ((2 * kk[None, :] + 1) * np.arange(2 * n)[:, None] % (8 * n)) / (8 * n)
    first = np.where(part[None, :] == 0, np.cos(angle), -np.sin(angle))
    run_tab = np.concatenate(halves(first), axis=0)

    kn = np.concatenate([k, k])
    partn = np.concatenate([np.zeros(n), np.ones(n)])
    angle = turn * ((2 * kn[:, None] + 1) * k[None, :] % (4 * n)) / (4 * n)
    chunk = np.where(partn[:, None] == 0, np.cos(angle), -np.sin(angle))
    high, low = halves(chunk)
    chunk_fwd = np.concatenate([high, low, high], axis=1)
    scale = 2.0 / extent
    high, low = halves(chunk.T * scale)
    chunk_inv = np.concatenate([high, low, high], axis=1)
    return second_tab, twist_tab, run_tab, np.ascontiguousarray(run_tab.T), chunk_fwd, chunk_inv


def dot(left, right):
    return lax.dot_general(left, right, (((1,), (0,)), ((), ())), preferred_element_type=F32)


def dot_nt(left, right):
    return lax.dot_general(left, right, (((1,), (1,)), ((), ())), preferred_element_type=F32)


def split(value):
    high = value.astype(BF16)
    return high, (value - high.astype(F32)).astype(BF16)


def partners(n, unit):
    ring = n // 2
    steps = [(half, low) for half in range(2) for low in range(ring) if half or low]
    return sorted(steps, key=lambda s: -(min(s[1], ring - s[1]) / unit + (3 - unit) * s[0]))


def moved(index, step, n):
    ring = n // 2
    half = lax.rem(index // ring + step[0], 2)
    return half * ring + lax.rem(lax.rem(index, ring) + step[1], ring)


def iota(shape, axis):
    return lax.broadcasted_iota(jnp.int32, shape, axis)


def kernel(
    n,
    slots,
    own,
    order,
    q_hbm, k_hbm, v_hbm, c_hbm, pos_hbm, grp_hbm, dec_hbm, res_hbm,
    sec_hbm, twi_hbm, run_hbm, runt_hbm, cfw_hbm, cin_hbm,
    out_ref, fg_ref,
    q_ref, k_ref, v_ref, c_ref, pos_ref, grp_ref, dec_ref, res_ref,
    sec_ref, twi_ref, run_ref, runt_ref, cfw_ref, cin_ref,
    x_send, x_recv, p_recv, c_send, c_recv, l_send, l_recv, f_send, f_recv,
    xs, taps, gcol, ys, onehot, unsort, lagsel,
    in_sem, x_ssem, x_rsem, p_ssem, p_rsem, c_ssem, c_rsem, l_ssem, l_rsem, f_sem,
):
    lanes = 128
    run = lanes // 2
    chans = n * slots
    ctx = lax.axis_index("ctx")
    ch = lax.axis_index("ch")

    sources = (grp_hbm, k_hbm, v_hbm, c_hbm, q_hbm, pos_hbm, dec_hbm, res_hbm,
               runt_hbm, run_hbm, cfw_hbm, twi_hbm, sec_hbm, cin_hbm)
    targets = (grp_ref, k_ref, v_ref, c_ref, q_ref, pos_ref, dec_ref, res_ref,
               runt_ref, run_ref, cfw_ref, twi_ref, sec_ref, cin_ref)
    loads = [
        pltpu.make_async_copy(source, target, in_sem.at[index])
        for index, (source, target) in enumerate(zip(sources, targets))
    ]
    for load in loads[:5]:
        load.start()
    ctx_steps = partners(n, 1)
    ch_steps = partners(n, 2)
    barrier = pltpu.get_barrier_semaphore()
    for step in ctx_steps:
        pl.semaphore_signal(
            barrier, inc=1, device_id={"ctx": moved(ctx, step, n)}, device_id_type=MESH
        )
    for load in loads[5:]:
        load.start()
    for step in ch_steps:
        pl.semaphore_signal(
            barrier, inc=1, device_id={"ch": moved(ch, step, n)}, device_id_type=MESH
        )

    loads[0].wait()
    if chans > lanes:
        per_row = chans // lanes
        pieces = [grp_ref[pl.ds(i, n, stride=per_row), :] for i in range(per_row)]
        group_all = jnp.concatenate(pieces, axis=1).astype(F32)
        pieces = [grp_ref[pl.ds(ch * per_row + i, 1), :] for i in range(per_row)]
        group_row = jnp.concatenate(pieces, axis=1).astype(F32)
    else:
        group_all = grp_ref[...].astype(F32)
        group_row = grp_ref[pl.ds(ch, 1), :].astype(F32)
    owner_row = jnp.floor(group_row * (1.0 / own))
    owner_rows = jnp.broadcast_to(owner_row, (chans, chans))
    owner_cols = jnp.transpose(owner_rows)
    row_i = iota((chans, chans), 0)
    col_i = iota((chans, chans), 1)
    same = owner_rows == owner_cols
    rank_row = jnp.sum(jnp.where(same & (row_i < col_i), 1.0, 0.0), axis=0, keepdims=True)
    rank_col = jnp.sum(jnp.where(same & (col_i < row_i), 1.0, 0.0), axis=1, keepdims=True)
    slot_row = owner_row * slots + rank_row
    slot_col = owner_cols[:, 0:1] * slots + rank_col
    sort = jnp.where(slot_row == row_i.astype(F32), 1.0, 0.0).astype(BF16)
    unsort[...] = jnp.where(slot_col == col_i.astype(F32), 1.0, 0.0).astype(BF16)

    for index in range(1, 5):
        loads[index].wait()
    gated = (k_ref[...].astype(F32) * v_ref[...].astype(F32)).astype(BF16)
    weighted = (c_ref[...].astype(F32) * q_ref[...].astype(F32)).astype(BF16)
    gated = dot(sort, gated).reshape(n, slots, lanes)
    weighted = dot(sort, weighted).reshape(n, slots, lanes)
    x_send[...] = jnp.concatenate([gated, weighted], axis=1).astype(BF16)
    loads[5].wait()

    pl.semaphore_wait(barrier, 2 * (n - 1))

    def pos_copy(target):
        return pltpu.make_async_remote_copy(
            src_ref=pos_ref, dst_ref=p_recv.at[ctx], send_sem=p_ssem, recv_sem=p_rsem,
            device_id={"ctx": target}, device_id_type=MESH,
        )

    def x_copy(target):
        return pltpu.make_async_remote_copy(
            src_ref=x_send.at[target], dst_ref=x_recv.at[ctx], send_sem=x_ssem, recv_sem=x_rsem,
            device_id={"ctx": target}, device_id_type=MESH,
        )

    def c_copy(target):
        return pltpu.make_async_remote_copy(
            src_ref=c_send.at[target], dst_ref=c_recv.at[ctx], send_sem=c_ssem, recv_sem=c_rsem,
            device_id={"ctx": target}, device_id_type=MESH,
        )

    flip = (1, n // 4)

    def l_copy(target):
        return pltpu.make_async_remote_copy(
            src_ref=l_send.at[moved(target, flip, n)], dst_ref=l_recv.at[ch],
            send_sem=l_ssem, recv_sem=l_rsem,
            device_id={"ch": target}, device_id_type=MESH,
        )

    def send_all(copy, me, steps):
        for step in steps:
            copy(moved(me, step, n)).start()

    def await_all(ref, sem):
        part = ref.at[pl.ds(0, n - 1)]
        pltpu.make_async_copy(part, part, sem).wait()

    send_all(pos_copy, ctx, ctx_steps)
    send_all(x_copy, ctx, ctx_steps)
    x_recv[ctx] = x_send[ctx]
    p_recv[ctx] = pos_ref[...]

    loads[6].wait()
    loads[7].wait()
    me_slot = iota((slots, chans), 0).astype(F32) + (ctx * slots).astype(F32)
    mine = jnp.where(slot_row == me_slot, group_row, 0.0)
    my_group = jnp.sum(mine, axis=1, keepdims=True)
    groups_total = dec_ref.shape[1]
    pick = my_group == iota((slots, groups_total), 1).astype(F32)
    rates, coefs = [], []
    for mode in range(order):
        rate = jnp.sum(jnp.where(pick, dec_ref[mode : mode + 1, :], 0.0), axis=1, keepdims=True)
        gain = jnp.sum(jnp.where(pick, res_ref[mode : mode + 1, :], 0.0), axis=1, keepdims=True)
        rates.append(jnp.broadcast_to(-rate, (slots, lanes)))
        coefs.append(jnp.broadcast_to(gain * jnp.sqrt(2.0 * rate), (slots, lanes)))
    lane_time = iota((slots, lanes), 1).astype(F32)

    def tap_step(chunk, carry):
        time = lane_time + (chunk * lanes).astype(F32)
        total = coefs[0] * jnp.exp(rates[0] * time)
        for mode in range(1, order):
            total = total + coefs[mode] * jnp.exp(rates[mode] * time)
        taps[pl.ds(pl.multiple_of(chunk * slots, slots), slots), :] = total
        return carry

    lax.fori_loop(0, n, tap_step, 0)

    for index in range(8, 14):
        loads[index].wait()

    def turned(real, imag, which):
        cos, sin = twi_ref[2 * which], twi_ref[2 * which + 1]
        return real * cos - imag * sin, real * sin + imag * cos

    def turned_back(real, imag, which):
        cos, sin = twi_ref[2 * which], twi_ref[2 * which + 1]
        return real * cos + imag * sin, imag * cos - real * sin

    def second(high, low, which):
        return (
            dot(high, sec_ref[2 * which])
            + dot(low, sec_ref[2 * which])
            + dot(high, sec_ref[2 * which + 1])
        )

    def second_back(high, low, which):
        return (
            dot_nt(high, sec_ref[2 * which])
            + dot_nt(low, sec_ref[2 * which])
            + dot_nt(high, sec_ref[2 * which + 1])
        )

    rows = []
    for i in range(slots):
        high, low = split(taps[pl.ds(i, n, stride=slots), :])
        mid = dot(cfw_ref[...], jnp.concatenate([high, high, low], axis=0))
        rows.append(jnp.concatenate(turned(mid[:n], mid[n:], 2), axis=1))
    high, low = split(jnp.concatenate(rows, axis=0))
    spec = second(high, low, 2)
    filt_re, filt_im = spec[:, :lanes], spec[:, lanes:]

    mine_all = jnp.floor(group_all * (1.0 / own)) == ctx.astype(F32)
    member = jnp.where(mine_all, 1.0, 0.0)
    before = jnp.where(row_i < col_i, 1.0, 0.0).astype(BF16)
    rank_all = dot(member.astype(BF16), before)
    for i in range(slots):
        hit = jnp.where(mine_all & (rank_all == float(i)), group_all, 0.0)
        gcol[pl.ds(i, n, stride=slots), :] = jnp.broadcast_to(
            jnp.sum(hit, axis=1, keepdims=True), (n, lanes)
        )
    first_own = (ctx * own).astype(F32)
    of_group = jnp.where(
        gcol[...] - first_own == iota((chans, lanes), 1).astype(F32), 1.0, 0.0
    )
    lagsel[...] = jnp.transpose(of_group)[: lagsel.shape[0], :].astype(BF16)

    await_all(p_recv, p_rsem)
    places = p_recv[...].reshape(n, lanes).astype(F32) * (1.0 / run)
    place = jnp.concatenate([places[:, 0:1], places[:, run : run + 1]], axis=0)
    place = jnp.concatenate([place, place + float(2 * n)], axis=0)
    onehot[...] = jnp.where(place == iota((4 * n, 4 * n), 1).astype(F32), 1.0, 0.0).astype(BF16)
    first = dot_nt(runt_ref[...], onehot[...]).astype(BF16)
    last = (dot(onehot[...], run_ref[...]) * (2.0 / (2 * lanes * n))).astype(BF16)
    last = jnp.concatenate([last[: 2 * n], last[2 * n :], last[: 2 * n]], axis=1)
    lane_i = iota((n, lanes), 1)
    left = lane_i < run

    await_all(x_recv, x_rsem)
    xs[...] = x_recv[...].astype(F32).reshape(2 * chans, lanes)
    gated_rows, weighted_rows = [[], []], [[], []]
    for i in range(slots):
        pair = []
        for row in (i, i + slots):
            value = xs[pl.ds(row, n, stride=2 * slots), :]
            both = jnp.concatenate(
                [jnp.where(left, value, 0.0), jnp.where(left, 0.0, value)], axis=0
            ).astype(BF16)
            pair.append(jnp.concatenate([both, both], axis=0))
        mid = dot(first, jnp.concatenate(pair, axis=1))
        for par in range(2):
            low_row = 2 * n * par
            for rows, off in ((gated_rows, 0), (weighted_rows, lanes)):
                piece = mid[low_row : low_row + 2 * n, off : off + lanes]
                rows[par].append(jnp.concatenate(turned(piece[:n], piece[n:], par), axis=1))

    def spectrum(rows):
        total = None
        for par in range(2):
            high, low = split(jnp.concatenate(rows[par], axis=0))
            term = second(high, low, par)
            total = term if total is None else total + term
        return total[:, :lanes], total[:, lanes:]

    gat_re, gat_im = spectrum(gated_rows)
    wei_re, wei_im = spectrum(weighted_rows)

    def channel(value, i):
        return value[i * n : (i + 1) * n]

    high, low = split(
        jnp.concatenate(
            [wei_re * gat_re + wei_im * gat_im, wei_im * gat_re - wei_re * gat_im], axis=1
        )
    )
    mid = second_back(high, low, 2)
    for i in range(slots):
        piece = channel(mid, i)
        high, low = split(
            jnp.concatenate(turned_back(piece[:, :lanes], piece[:, lanes:], 2), axis=0)
        )
        ys[pl.ds(i, n, stride=slots), :] = dot(
            cin_ref[...], jnp.concatenate([high, high, low], axis=0)
        )
    l_send[...] = ys[...].reshape(n, slots, lanes).astype(BF16)
    send_all(l_copy, ch, ch_steps)
    l_recv[ch] = l_send[moved(ch, flip, n)]

    high, low = split(
        jnp.concatenate(
            [filt_re * gat_re - filt_im * gat_im, filt_re * gat_im + filt_im * gat_re], axis=1
        )
    )
    mids = [second_back(high, low, par) for par in range(2)]
    for i in range(slots):
        stack = []
        for par in range(2):
            piece = channel(mids[par], i)
            stack += list(turned_back(piece[:, :lanes], piece[:, lanes:], par))
        high, low = split(jnp.concatenate(stack, axis=0))
        value = dot(last, jnp.concatenate([high, high, low], axis=0))
        ys[pl.ds(i, n, stride=slots), :] = jnp.where(left, value[:n], value[n:])
    c_send[...] = ys[...].reshape(n, slots, lanes).astype(BF16)
    send_all(c_copy, ctx, ctx_steps)
    c_recv[ctx] = c_send[ctx]

    await_all(p_recv, p_ssem)
    await_all(x_send, x_ssem)
    await_all(l_recv, l_rsem)
    sums = dot(lagsel[...], l_recv[...].astype(F32).reshape(chans, lanes).astype(BF16))
    f_send[...] = sums[: f_send.shape[0]]
    far = pltpu.make_async_remote_copy(
        src_ref=f_send, dst_ref=f_recv, send_sem=f_sem.at[0], recv_sem=f_sem.at[1],
        device_id={"ctx": moved(ch, flip, n), "ch": ctx}, device_id_type=MESH,
    )
    far.start()

    await_all(l_send, l_ssem)
    await_all(c_recv, c_rsem)
    conv = dot(unsort[...], c_recv[...].astype(F32).reshape(chans, lanes).astype(BF16))
    out_ref[...] = (q_ref[...].astype(F32) * conv).astype(BF16)

    await_all(c_send, c_ssem)
    far.wait()
    fg_ref[...] = f_recv[...]


def shards(query_proj, key_proj, value_proj, cotangent, positions, group_of, decay_rates, residues):
    n = lax.axis_size("ctx")
    chans, lanes = query_proj.shape
    slots = chans // n
    groups_total, order = decay_rates.shape
    own = groups_total // lax.axis_size("ch")
    own_pad = -(-own // 16) * 16
    width = min(chans, lanes)
    tables = make_tables(n, lanes)
    args = (
        query_proj, key_proj, value_proj, cotangent,
        positions.reshape(1, lanes), group_of.reshape(-1, width),
        decay_rates.T, residues.T,
    ) + tuple(jnp.asarray(table) for table in tables)
    any_spec = pl.BlockSpec(memory_space=pl.ANY)
    vmem_spec = pl.BlockSpec(memory_space=pltpu.VMEM)
    dma = pltpu.SemaphoreType.DMA
    return pl.pallas_call(
        functools.partial(kernel, n, slots, own, order),
        out_shape=(
            pltpu.VMEM((chans, lanes), BF16),
            pltpu.VMEM((own, lanes), F32),
        ),
        in_specs=[any_spec] * len(args),
        out_specs=(vmem_spec, vmem_spec),
        scratch_shapes=[pltpu.VMEM(arg.shape, arg.dtype) for arg in args]
        + [
            pltpu.VMEM((n, 2 * slots, lanes), BF16),
            pltpu.VMEM((n, 2 * slots, lanes), BF16),
            pltpu.VMEM((n, 1, lanes), jnp.int32),
            pltpu.VMEM((n, slots, lanes), BF16),
            pltpu.VMEM((n, slots, lanes), BF16),
            pltpu.VMEM((n, slots, lanes), BF16),
            pltpu.VMEM((n, slots, lanes), BF16),
            pltpu.VMEM((own, lanes), F32),
            pltpu.VMEM((own, lanes), F32),
            pltpu.VMEM((2 * chans, lanes), F32),
            pltpu.VMEM((chans, lanes), F32),
            pltpu.VMEM((chans, lanes), F32),
            pltpu.VMEM((chans, lanes), F32),
            pltpu.VMEM((4 * n, 4 * n), BF16),
            pltpu.VMEM((chans, chans), BF16),
            pltpu.VMEM((own_pad, chans), BF16),
            dma((len(args),)),
            dma(()), dma(()), dma(()), dma(()),
            dma(()), dma(()), dma(()), dma(()),
            dma((2,)),
        ],
        compiler_params=pltpu.CompilerParams(collective_id=0, has_side_effects=True),
    )(*args)


def solution(mesh):
    placed = (
        P("ch", "ctx"),
        P("ch", "ctx"),
        P("ch", "ctx"),
        P("ch", "ctx"),
        P("ctx"),
        P(),
        P(),
        P(),
    )
    return jax.shard_map(
        shards,
        mesh=mesh,
        in_specs=placed,
        out_specs=(P("ch", "ctx"), P("ch", "ctx")),
        check_vma=False,
    )
```

```python
import functools
import math

import jax
import jax.numpy as jnp
import ml_dtypes
import numpy as np
from jax import lax
from jax.experimental import pallas as pl
from jax.experimental.pallas import tpu as pltpu
from jax.sharding import PartitionSpec as P

MESH = pl.DeviceIdType.MESH
BF16 = jnp.bfloat16
F32 = jnp.float32


def halves(table):
    high = table.astype(ml_dtypes.bfloat16)
    low = (table - high.astype(np.float64)).astype(ml_dtypes.bfloat16)
    return high, low


def make_tables(n, lanes):
    run = lanes // 2
    extent = 2 * lanes * n
    turn = 2.0 * math.pi
    k = np.arange(n)
    j = np.arange(lanes) % run
    m = np.arange(lanes) % run
    par = np.arange(lanes) // run

    def second(angle, mask):
        cos, sin = np.cos(angle) * mask, np.sin(angle) * mask
        return np.block([[cos, -sin], [sin, cos]])

    perm_angle = turn * (j[:, None] * m[None, :] % run) / run
    nat_angle = turn * (np.arange(lanes)[:, None] * (2 * m + par)[None, :] % lanes) / lanes
    seconds = [second(perm_angle, (par == p)[None, :].astype(np.float64)) for p in range(2)]
    seconds.append(second(nat_angle, 1.0))
    second_tab = np.stack([part for table in seconds for part in halves(table)])

    twists = []
    for rows, cols in ((k, j), (k + 2 * n, j), (k, np.arange(lanes))):
        angle = turn * ((2 * rows[:, None] + 1) * cols[None, :] % (2 * extent)) / (2 * extent)
        twists += [np.cos(angle), -np.sin(angle)]
    twist_tab = np.stack(twists).astype(np.float32)

    kk = np.concatenate([k, k, k + 2 * n, k + 2 * n])
    part = np.concatenate([np.zeros(n), np.ones(n)] * 2)
    angle = turn * ((2 * kk[None, :] + 1) * np.arange(2 * n)[:, None] % (8 * n)) / (8 * n)
    first = np.where(part[None, :] == 0, np.cos(angle), -np.sin(angle))
    run_tab = np.concatenate(halves(first), axis=0)

    kn = np.concatenate([k, k])
    partn = np.concatenate([np.zeros(n), np.ones(n)])
    angle = turn * ((2 * kn[:, None] + 1) * k[None, :] % (4 * n)) / (4 * n)
    chunk = np.where(partn[:, None] == 0, np.cos(angle), -np.sin(angle))
    high, low = halves(chunk)
    chunk_fwd = np.concatenate([high, low, high], axis=1)
    scale = 2.0 / extent
    high, low = halves(chunk.T * scale)
    chunk_inv = np.concatenate([high, low, high], axis=1)
    return second_tab, twist_tab, run_tab, np.ascontiguousarray(run_tab.T), chunk_fwd, chunk_inv


def dot(left, right):
    return lax.dot_general(left, right, (((1,), (0,)), ((), ())), preferred_element_type=F32)


def dot_nt(left, right):
    return lax.dot_general(left, right, (((1,), (1,)), ((), ())), preferred_element_type=F32)


def split(value):
    high = value.astype(BF16)
    return high, (value - high.astype(F32)).astype(BF16)


def partners(n, unit):
    ring = n // 2
    steps = [(half, low) for half in range(2) for low in range(ring) if half or low]
    return sorted(steps, key=lambda s: -(min(s[1], ring - s[1]) / unit + (3 - unit) * s[0]))


def moved(index, step, n):
    ring = n // 2
    return ((index + step[0] * ring) & ring) + ((index + step[1]) & (ring - 1))


def iota(shape, axis):
    return lax.broadcasted_iota(jnp.int32, shape, axis)


def kernel(
    n,
    slots,
    own,
    order,
    q_hbm, k_hbm, v_hbm, c_hbm, pos_hbm, grp_hbm, dec_hbm, res_hbm,
    sec_hbm, twi_hbm, run_hbm, runt_hbm, cfw_hbm, cin_hbm,
    out_ref, fg_ref,
    q_ref, k_ref, v_ref, c_ref, pos_ref, grp_ref, dec_ref, res_ref,
    sec_ref, twi_ref, run_ref, runt_ref, cfw_ref, cin_ref,
    x_send, x_recv, p_recv, c_send, c_recv, l_send, l_recv, f_send, f_recv,
    xs, taps, gcol, ys, onehot, unsort, lagsel,
    in_sem, x_ssem, x_rsem, p_ssem, p_rsem, c_ssem, c_rsem, l_ssem, l_rsem, f_sem,
):
    lanes = 128
    run = lanes // 2
    chans = n * slots
    ctx = lax.axis_index("ctx")
    ch = lax.axis_index("ch")

    sources = (grp_hbm, k_hbm, v_hbm, c_hbm, q_hbm, pos_hbm, dec_hbm, res_hbm,
               runt_hbm, run_hbm, cfw_hbm, twi_hbm, sec_hbm, cin_hbm)
    targets = (grp_ref, k_ref, v_ref, c_ref, q_ref, pos_ref, dec_ref, res_ref,
               runt_ref, run_ref, cfw_ref, twi_ref, sec_ref, cin_ref)
    loads = [
        pltpu.make_async_copy(source, target, in_sem.at[index])
        for index, (source, target) in enumerate(zip(sources, targets))
    ]
    ctx_steps = partners(n, 1)
    ch_steps = partners(n, 2)
    barrier = pltpu.get_barrier_semaphore()
    for step in ctx_steps:
        pl.semaphore_signal(
            barrier, inc=1, device_id={"ctx": moved(ctx, step, n)}, device_id_type=MESH
        )
    for load in loads:
        load.start()
    for step in ch_steps:
        pl.semaphore_signal(
            barrier, inc=1, device_id={"ch": moved(ch, step, n)}, device_id_type=MESH
        )

    loads[0].wait()
    if chans > lanes:
        per_row = chans // lanes
        pieces = [grp_ref[pl.ds(i, n, stride=per_row), :] for i in range(per_row)]
        group_all = jnp.concatenate(pieces, axis=1).astype(F32)
        pieces = [grp_ref[pl.ds(ch * per_row + i, 1), :] for i in range(per_row)]
        group_row = jnp.concatenate(pieces, axis=1).astype(F32)
    else:
        group_all = grp_ref[...].astype(F32)
        group_row = grp_ref[pl.ds(ch, 1), :].astype(F32)
    owner_row = jnp.floor(group_row * (1.0 / own))
    owner_rows = jnp.broadcast_to(owner_row, (chans, chans))
    owner_cols = jnp.transpose(owner_rows)
    row_i = iota((chans, chans), 0)
    col_i = iota((chans, chans), 1)
    same = owner_rows == owner_cols
    rank_row = jnp.sum(jnp.where(same & (row_i < col_i), 1.0, 0.0), axis=0, keepdims=True)
    rank_col = jnp.sum(jnp.where(same & (col_i < row_i), 1.0, 0.0), axis=1, keepdims=True)
    slot_row = owner_row * slots + rank_row
    slot_col = owner_cols[:, 0:1] * slots + rank_col
    sort = jnp.where(slot_row == row_i.astype(F32), 1.0, 0.0).astype(BF16)
    unsort[...] = jnp.where(slot_col == col_i.astype(F32), 1.0, 0.0).astype(BF16)

    for index in range(1, 5):
        loads[index].wait()
    gated = (k_ref[...].astype(F32) * v_ref[...].astype(F32)).astype(BF16)
    weighted = (c_ref[...].astype(F32) * q_ref[...].astype(F32)).astype(BF16)
    gated = dot(sort, gated).reshape(n, slots, lanes)
    weighted = dot(sort, weighted).reshape(n, slots, lanes)
    x_send[...] = jnp.concatenate([gated, weighted], axis=1).astype(BF16)
    loads[5].wait()

    pl.semaphore_wait(barrier, 2 * (n - 1))

    def pos_copy(target):
        return pltpu.make_async_remote_copy(
            src_ref=pos_ref, dst_ref=p_recv.at[ctx], send_sem=p_ssem, recv_sem=p_rsem,
            device_id={"ctx": target}, device_id_type=MESH,
        )

    def x_copy(target):
        return pltpu.make_async_remote_copy(
            src_ref=x_send.at[target], dst_ref=x_recv.at[ctx], send_sem=x_ssem, recv_sem=x_rsem,
            device_id={"ctx": target}, device_id_type=MESH,
        )

    def c_copy(target):
        return pltpu.make_async_remote_copy(
            src_ref=c_send.at[target], dst_ref=c_recv.at[ctx], send_sem=c_ssem, recv_sem=c_rsem,
            device_id={"ctx": target}, device_id_type=MESH,
        )

    flip = (1, n // 4)

    def l_copy(target):
        return pltpu.make_async_remote_copy(
            src_ref=l_send.at[moved(target, flip, n)], dst_ref=l_recv.at[ch],
            send_sem=l_ssem, recv_sem=l_rsem,
            device_id={"ch": target}, device_id_type=MESH,
        )

    def send_all(copy, me, steps):
        for step in steps:
            copy(moved(me, step, n)).start()

    def await_all(ref, sem):
        part = ref.at[pl.ds(0, n - 1)]
        pltpu.make_async_copy(part, part, sem).wait()

    send_all(pos_copy, ctx, ctx_steps)
    send_all(x_copy, ctx, ctx_steps)
    x_recv[ctx] = x_send[ctx]
    p_recv[ctx] = pos_ref[...]

    loads[6].wait()
    loads[7].wait()
    me_slot = iota((slots, chans), 0).astype(F32) + (ctx * slots).astype(F32)
    mine = jnp.where(slot_row == me_slot, group_row, 0.0)
    my_group = jnp.sum(mine, axis=1, keepdims=True)
    groups_total = dec_ref.shape[1]
    pick = my_group == iota((slots, groups_total), 1).astype(F32)
    rates, coefs = [], []
    for mode in range(order):
        rate = jnp.sum(jnp.where(pick, dec_ref[mode : mode + 1, :], 0.0), axis=1, keepdims=True)
        gain = jnp.sum(jnp.where(pick, res_ref[mode : mode + 1, :], 0.0), axis=1, keepdims=True)
        rates.append(jnp.broadcast_to(-rate, (slots, lanes)))
        coefs.append(jnp.broadcast_to(gain * jnp.sqrt(2.0 * rate), (slots, lanes)))
    lane_time = iota((slots, lanes), 1).astype(F32)

    def tap_step(chunk, carry):
        time = lane_time + (chunk * lanes).astype(F32)
        total = coefs[0] * jnp.exp(rates[0] * time)
        for mode in range(1, order):
            total = total + coefs[mode] * jnp.exp(rates[mode] * time)
        taps[pl.ds(pl.multiple_of(chunk * slots, slots), slots), :] = total
        return carry

    lax.fori_loop(0, n, tap_step, 0)

    for index in range(8, 14):
        loads[index].wait()

    def turned(real, imag, which):
        cos, sin = twi_ref[2 * which], twi_ref[2 * which + 1]
        return real * cos - imag * sin, real * sin + imag * cos

    def turned_back(real, imag, which):
        cos, sin = twi_ref[2 * which], twi_ref[2 * which + 1]
        return real * cos + imag * sin, imag * cos - real * sin

    def second(high, low, which):
        return (
            dot(high, sec_ref[2 * which])
            + dot(low, sec_ref[2 * which])
            + dot(high, sec_ref[2 * which + 1])
        )

    def second_back(high, low, which):
        return (
            dot_nt(high, sec_ref[2 * which])
            + dot_nt(low, sec_ref[2 * which])
            + dot_nt(high, sec_ref[2 * which + 1])
        )

    rows = []
    for i in range(slots):
        high, low = split(taps[pl.ds(i, n, stride=slots), :])
        mid = dot(cfw_ref[...], jnp.concatenate([high, high, low], axis=0))
        rows.append(jnp.concatenate(turned(mid[:n], mid[n:], 2), axis=1))
    high, low = split(jnp.concatenate(rows, axis=0))
    spec = second(high, low, 2)
    filt_re, filt_im = spec[:, :lanes], spec[:, lanes:]

    mine_all = jnp.floor(group_all * (1.0 / own)) == ctx.astype(F32)
    member = jnp.where(mine_all, 1.0, 0.0)
    before = jnp.where(row_i < col_i, 1.0, 0.0).astype(BF16)
    rank_all = dot(member.astype(BF16), before)
    for i in range(slots):
        hit = jnp.where(mine_all & (rank_all == float(i)), group_all, 0.0)
        gcol[pl.ds(i, n, stride=slots), :] = jnp.broadcast_to(
            jnp.sum(hit, axis=1, keepdims=True), (n, lanes)
        )
    first_own = (ctx * own).astype(F32)
    of_group = jnp.where(
        gcol[...] - first_own == iota((chans, lanes), 1).astype(F32), 1.0, 0.0
    )
    lagsel[...] = jnp.transpose(of_group)[: lagsel.shape[0], :].astype(BF16)

    await_all(p_recv, p_rsem)
    places = p_recv[...].reshape(n, lanes).astype(F32) * (1.0 / run)
    place = jnp.concatenate([places[:, 0:1], places[:, run : run + 1]], axis=0)
    place = jnp.concatenate([place, place + float(2 * n)], axis=0)
    onehot[...] = jnp.where(place == iota((4 * n, 4 * n), 1).astype(F32), 1.0, 0.0).astype(BF16)
    first = dot_nt(runt_ref[...], onehot[...]).astype(BF16)
    last = (dot(onehot[...], run_ref[...]) * (2.0 / (2 * lanes * n))).astype(BF16)
    last = jnp.concatenate([last[: 2 * n], last[2 * n :], last[: 2 * n]], axis=1)
    lane_i = iota((n, lanes), 1)
    left = lane_i < run

    await_all(x_recv, x_rsem)
    xs[...] = x_recv[...].astype(F32).reshape(2 * chans, lanes)
    gated_rows, weighted_rows = [[], []], [[], []]
    for i in range(slots):
        pair = []
        for row in (i, i + slots):
            value = xs[pl.ds(row, n, stride=2 * slots), :]
            both = jnp.concatenate(
                [jnp.where(left, value, 0.0), jnp.where(left, 0.0, value)], axis=0
            ).astype(BF16)
            pair.append(jnp.concatenate([both, both], axis=0))
        mid = dot(first, jnp.concatenate(pair, axis=1))
        for par in range(2):
            low_row = 2 * n * par
            for rows, off in ((gated_rows, 0), (weighted_rows, lanes)):
                piece = mid[low_row : low_row + 2 * n, off : off + lanes]
                rows[par].append(jnp.concatenate(turned(piece[:n], piece[n:], par), axis=1))

    def spectrum(rows):
        total = None
        for par in range(2):
            high, low = split(jnp.concatenate(rows[par], axis=0))
            term = second(high, low, par)
            total = term if total is None else total + term
        return total[:, :lanes], total[:, lanes:]

    gat_re, gat_im = spectrum(gated_rows)
    wei_re, wei_im = spectrum(weighted_rows)

    def channel(value, i):
        return value[i * n : (i + 1) * n]

    high, low = split(
        jnp.concatenate(
            [wei_re * gat_re + wei_im * gat_im, wei_im * gat_re - wei_re * gat_im], axis=1
        )
    )
    mid = second_back(high, low, 2)
    for i in range(slots):
        piece = channel(mid, i)
        high, low = split(
            jnp.concatenate(turned_back(piece[:, :lanes], piece[:, lanes:], 2), axis=0)
        )
        ys[pl.ds(i, n, stride=slots), :] = dot(
            cin_ref[...], jnp.concatenate([high, high, low], axis=0)
        )
    l_send[...] = ys[...].reshape(n, slots, lanes).astype(BF16)
    send_all(l_copy, ch, ch_steps)
    l_recv[ch] = l_send[moved(ch, flip, n)]

    high, low = split(
        jnp.concatenate(
            [filt_re * gat_re - filt_im * gat_im, filt_re * gat_im + filt_im * gat_re], axis=1
        )
    )
    mids = [second_back(high, low, par) for par in range(2)]
    for i in range(slots):
        stack = []
        for par in range(2):
            piece = channel(mids[par], i)
            stack += list(turned_back(piece[:, :lanes], piece[:, lanes:], par))
        high, low = split(jnp.concatenate(stack, axis=0))
        value = dot(last, jnp.concatenate([high, high, low], axis=0))
        ys[pl.ds(i, n, stride=slots), :] = jnp.where(left, value[:n], value[n:])
    c_send[...] = ys[...].reshape(n, slots, lanes).astype(BF16)
    send_all(c_copy, ctx, ctx_steps)
    c_recv[ctx] = c_send[ctx]

    await_all(p_recv, p_ssem)
    await_all(x_send, x_ssem)
    await_all(l_recv, l_rsem)
    sums = dot(lagsel[...], l_recv[...].astype(F32).reshape(chans, lanes).astype(BF16))
    f_send[...] = sums[: f_send.shape[0]]
    far = pltpu.make_async_remote_copy(
        src_ref=f_send, dst_ref=f_recv, send_sem=f_sem.at[0], recv_sem=f_sem.at[1],
        device_id={"ctx": moved(ch, flip, n), "ch": ctx}, device_id_type=MESH,
    )
    far.start()

    await_all(l_send, l_ssem)
    await_all(c_recv, c_rsem)
    conv = dot(unsort[...], c_recv[...].astype(F32).reshape(chans, lanes).astype(BF16))
    out_ref[...] = (q_ref[...].astype(F32) * conv).astype(BF16)

    await_all(c_send, c_ssem)
    far.wait()
    fg_ref[...] = f_recv[...]


def put_kernel(out_ref, fg_ref, out_hbm, fg_hbm, sem):
    puts = [
        pltpu.make_async_copy(out_ref, out_hbm, sem.at[0]),
        pltpu.make_async_copy(fg_ref, fg_hbm, sem.at[1]),
    ]
    for put in puts:
        put.start()
    for put in puts:
        put.wait()


def shards(query_proj, key_proj, value_proj, cotangent, positions, group_of, decay_rates, residues):
    n = lax.axis_size("ctx")
    chans, lanes = query_proj.shape
    slots = chans // n
    groups_total, order = decay_rates.shape
    own = groups_total // lax.axis_size("ch")
    own_pad = -(-own // 16) * 16
    width = min(chans, lanes)
    tables = make_tables(n, lanes)
    args = (
        query_proj, key_proj, value_proj, cotangent,
        positions.reshape(1, lanes), group_of.reshape(-1, width),
        decay_rates.T, residues.T,
    ) + tuple(jnp.asarray(table) for table in tables)
    any_spec = pl.BlockSpec(memory_space=pl.ANY)
    vmem_spec = pl.BlockSpec(memory_space=pltpu.VMEM)
    dma = pltpu.SemaphoreType.DMA
    output, filter_grad = pl.pallas_call(
        functools.partial(kernel, n, slots, own, order),
        out_shape=(
            pltpu.VMEM((chans, lanes), BF16),
            pltpu.VMEM((own, lanes), F32),
        ),
        in_specs=[any_spec] * len(args),
        out_specs=(vmem_spec, vmem_spec),
        scratch_shapes=[pltpu.VMEM(arg.shape, arg.dtype) for arg in args]
        + [
            pltpu.VMEM((n, 2 * slots, lanes), BF16),
            pltpu.VMEM((n, 2 * slots, lanes), BF16),
            pltpu.VMEM((n, 1, lanes), jnp.int32),
            pltpu.VMEM((n, slots, lanes), BF16),
            pltpu.VMEM((n, slots, lanes), BF16),
            pltpu.VMEM((n, slots, lanes), BF16),
            pltpu.VMEM((n, slots, lanes), BF16),
            pltpu.VMEM((own, lanes), F32),
            pltpu.VMEM((own, lanes), F32),
            pltpu.VMEM((2 * chans, lanes), F32),
            pltpu.VMEM((chans, lanes), F32),
            pltpu.VMEM((chans, lanes), F32),
            pltpu.VMEM((chans, lanes), F32),
            pltpu.VMEM((4 * n, 4 * n), BF16),
            pltpu.VMEM((chans, chans), BF16),
            pltpu.VMEM((own_pad, chans), BF16),
            dma((len(args),)),
            dma(()), dma(()), dma(()), dma(()),
            dma(()), dma(()), dma(()), dma(()),
            dma((2,)),
        ],
        compiler_params=pltpu.CompilerParams(collective_id=0, has_side_effects=True),
    )(*args)
    return pl.pallas_call(
        put_kernel,
        out_shape=(
            jax.ShapeDtypeStruct((chans, lanes), BF16),
            jax.ShapeDtypeStruct((own, lanes), F32),
        ),
        in_specs=[vmem_spec, vmem_spec],
        out_specs=(any_spec, any_spec),
        scratch_shapes=[dma((2,))],
    )(
        pltpu.with_memory_space_constraint(output, pltpu.VMEM),
        pltpu.with_memory_space_constraint(filter_grad, pltpu.VMEM),
    )


def solution(mesh):
    placed = (
        P("ch", "ctx"),
        P("ch", "ctx"),
        P("ch", "ctx"),
        P("ch", "ctx"),
        P("ctx"),
        P(),
        P(),
        P(),
    )
    return jax.shard_map(
        shards,
        mesh=mesh,
        in_specs=placed,
        out_specs=(P("ch", "ctx"), P("ch", "ctx")),
        check_vma=False,
    )
```

```python
import functools
import math

import jax
import jax.numpy as jnp
import ml_dtypes
import numpy as np
from jax import lax
from jax.experimental import pallas as pl
from jax.experimental.pallas import tpu as pltpu
from jax.sharding import PartitionSpec as P

MESH = pl.DeviceIdType.MESH
BF16 = jnp.bfloat16
F32 = jnp.float32


def halves(table):
    high = table.astype(ml_dtypes.bfloat16)
    low = (table - high.astype(np.float64)).astype(ml_dtypes.bfloat16)
    return high, low


def make_tables(n, lanes):
    run = lanes // 2
    extent = 2 * lanes * n
    turn = 2.0 * math.pi
    k = np.arange(n)
    j = np.arange(lanes) % run
    m = np.arange(run)

    def second(angle):
        cos, sin = np.cos(angle), np.sin(angle)
        return np.block([[cos, -sin], [sin, cos]])

    perm = second(turn * (j[:, None] * m[None, :] % run) / run)
    lane = np.arange(lanes)
    nat = [
        second(turn * (lane[:, None] * (2 * m + p)[None, :] % lanes) / lanes) for p in range(2)
    ]
    second_tab = np.stack(
        [np.concatenate(halves(perm), axis=1), *halves(np.concatenate(nat, axis=1))]
    )

    twists = []
    for rows, cols in ((k, j), (k + 2 * n, j), (k, np.arange(lanes))):
        angle = turn * ((2 * rows[:, None] + 1) * cols[None, :] % (2 * extent)) / (2 * extent)
        twists += [np.cos(angle), -np.sin(angle)]
    twist_tab = np.stack(twists).astype(np.float32)

    kk = np.concatenate([k, k, k + 2 * n, k + 2 * n])
    part = np.concatenate([np.zeros(n), np.ones(n)] * 2)
    angle = turn * ((2 * kk[None, :] + 1) * np.arange(2 * n)[:, None] % (8 * n)) / (8 * n)
    first = np.where(part[None, :] == 0, np.cos(angle), -np.sin(angle))
    run_tab = np.concatenate(halves(first), axis=0)

    kn = np.concatenate([k, k])
    partn = np.concatenate([np.zeros(n), np.ones(n)])
    angle = turn * ((2 * kn[:, None] + 1) * k[None, :] % (4 * n)) / (4 * n)
    chunk = np.where(partn[:, None] == 0, np.cos(angle), -np.sin(angle))
    high, low = halves(chunk)
    chunk_fwd = np.concatenate([high, low, high], axis=1)
    scale = 2.0 / extent
    high, low = halves(chunk.T * scale)
    chunk_inv = np.concatenate([high, low, high], axis=1)
    return second_tab, twist_tab, run_tab, np.ascontiguousarray(run_tab.T), chunk_fwd, chunk_inv


def dot(left, right):
    return lax.dot_general(left, right, (((1,), (0,)), ((), ())), preferred_element_type=F32)


def dot_nt(left, right):
    return lax.dot_general(left, right, (((1,), (1,)), ((), ())), preferred_element_type=F32)


def split(value):
    high = value.astype(BF16)
    return high, (value - high.astype(F32)).astype(BF16)


def partners(n, unit):
    ring = n // 2
    steps = [(half, low) for half in range(2) for low in range(ring) if half or low]
    return sorted(steps, key=lambda s: -(min(s[1], ring - s[1]) / unit + (3 - unit) * s[0]))


def moved(index, step, n):
    ring = n // 2
    return ((index + step[0] * ring) & ring) + ((index + step[1]) & (ring - 1))


def iota(shape, axis):
    return lax.broadcasted_iota(jnp.int32, shape, axis)


def kernel(
    n,
    slots,
    own,
    order,
    q_hbm, k_hbm, v_hbm, c_hbm, pos_hbm, grp_hbm, dec_hbm, res_hbm,
    sec_hbm, twi_hbm, run_hbm, runt_hbm, cfw_hbm, cin_hbm,
    out_ref, fg_ref,
    q_ref, k_ref, v_ref, c_ref, pos_ref, grp_ref, dec_ref, res_ref,
    sec_ref, twi_ref, run_ref, runt_ref, cfw_ref, cin_ref,
    x_send, x_recv, p_recv, c_send, c_recv, l_send, l_recv, f_send, f_recv,
    xs, taps, gcol, ys, onehot, unsort, lagsel,
    in_sem, x_ssem, x_rsem, p_ssem, p_rsem, c_ssem, c_rsem, l_ssem, l_rsem, f_sem,
):
    lanes = 128
    run = lanes // 2
    chans = n * slots
    ctx = lax.axis_index("ctx")
    ch = lax.axis_index("ch")

    sources = (grp_hbm, k_hbm, v_hbm, c_hbm, q_hbm, pos_hbm, dec_hbm, res_hbm,
               runt_hbm, run_hbm, cfw_hbm, twi_hbm, sec_hbm, cin_hbm)
    targets = (grp_ref.at[pl.ds(0, grp_hbm.shape[0])], k_ref, v_ref, c_ref, q_ref, pos_ref, dec_ref, res_ref,
               runt_ref, run_ref, cfw_ref, twi_ref, sec_ref, cin_ref)
    loads = [
        pltpu.make_async_copy(source, target, in_sem.at[index])
        for index, (source, target) in enumerate(zip(sources, targets))
    ]
    ctx_steps = partners(n, 1)
    ch_steps = partners(n, 2)
    barrier = pltpu.get_barrier_semaphore()
    for step in ctx_steps:
        pl.semaphore_signal(
            barrier, inc=1, device_id={"ctx": moved(ctx, step, n)}, device_id_type=MESH
        )
    for load in loads:
        load.start()
    for step in ch_steps:
        pl.semaphore_signal(
            barrier, inc=1, device_id={"ch": moved(ch, step, n)}, device_id_type=MESH
        )

    loads[0].wait()
    if chans > lanes:
        per_row = chans // lanes
        pieces = [grp_ref[pl.ds(i, n, stride=per_row), :] for i in range(per_row)]
        group_all = jnp.concatenate(pieces, axis=1).astype(F32)
        pieces = [grp_ref[pl.ds(ch * per_row + i, 1), :] for i in range(per_row)]
        group_row = jnp.concatenate(pieces, axis=1).astype(F32)
    else:
        group_all = grp_ref[:n, :].astype(F32)
        group_row = grp_ref[pl.ds(ch, 1), :].astype(F32)
    owner_row = jnp.floor(group_row * (1.0 / own))
    owner_rows = jnp.broadcast_to(owner_row, (chans, chans))
    owner_cols = jnp.transpose(owner_rows)
    row_i = iota((chans, chans), 0)
    col_i = iota((chans, chans), 1)
    same = owner_rows == owner_cols
    rank_row = jnp.sum(jnp.where(same & (row_i < col_i), 1.0, 0.0), axis=0, keepdims=True)
    rank_col = jnp.sum(jnp.where(same & (col_i < row_i), 1.0, 0.0), axis=1, keepdims=True)
    slot_row = owner_row * slots + rank_row
    slot_col = owner_cols[:, 0:1] * slots + rank_col
    sort = jnp.where(slot_row == row_i.astype(F32), 1.0, 0.0).astype(BF16)
    unsort[...] = jnp.where(slot_col == col_i.astype(F32), 1.0, 0.0).astype(BF16)

    for index in range(1, 5):
        loads[index].wait()
    gated = (k_ref[...].astype(F32) * v_ref[...].astype(F32)).astype(BF16)
    weighted = (c_ref[...].astype(F32) * q_ref[...].astype(F32)).astype(BF16)
    gated = dot(sort, gated).reshape(n, slots, lanes)
    weighted = dot(sort, weighted).reshape(n, slots, lanes)
    x_send[...] = jnp.concatenate([gated, weighted], axis=1).astype(BF16)
    loads[5].wait()

    pl.semaphore_wait(barrier, 2 * (n - 1))

    def pos_copy(target):
        return pltpu.make_async_remote_copy(
            src_ref=pos_ref, dst_ref=p_recv.at[ctx], send_sem=p_ssem, recv_sem=p_rsem,
            device_id={"ctx": target}, device_id_type=MESH,
        )

    def x_copy(target):
        return pltpu.make_async_remote_copy(
            src_ref=x_send.at[target], dst_ref=x_recv.at[ctx], send_sem=x_ssem, recv_sem=x_rsem,
            device_id={"ctx": target}, device_id_type=MESH,
        )

    def c_copy(target):
        return pltpu.make_async_remote_copy(
            src_ref=c_send.at[target], dst_ref=c_recv.at[ctx], send_sem=c_ssem, recv_sem=c_rsem,
            device_id={"ctx": target}, device_id_type=MESH,
        )

    flip = (1, n // 4)

    def l_copy(target):
        return pltpu.make_async_remote_copy(
            src_ref=l_send.at[moved(target, flip, n)], dst_ref=l_recv.at[ch],
            send_sem=l_ssem, recv_sem=l_rsem,
            device_id={"ch": target}, device_id_type=MESH,
        )

    def send_all(copy, me, steps):
        for step in steps:
            copy(moved(me, step, n)).start()

    def await_all(ref, sem):
        part = ref.at[pl.ds(0, n - 1)]
        pltpu.make_async_copy(part, part, sem).wait()

    for step in ctx_steps:
        pos_copy(moved(ctx, step, n)).start()
        x_copy(moved(ctx, step, n)).start()
    x_recv[ctx] = x_send[ctx]
    p_recv[ctx] = pos_ref[...]

    loads[6].wait()
    loads[7].wait()
    me_slot = iota((slots, chans), 0).astype(F32) + (ctx * slots).astype(F32)
    mine = jnp.where(slot_row == me_slot, group_row, 0.0)
    my_group = jnp.sum(mine, axis=1, keepdims=True)
    groups_total = dec_ref.shape[1]
    pick = my_group == iota((slots, groups_total), 1).astype(F32)
    rates, coefs = [], []
    for mode in range(order):
        rate = jnp.sum(jnp.where(pick, dec_ref[mode : mode + 1, :], 0.0), axis=1, keepdims=True)
        gain = jnp.sum(jnp.where(pick, res_ref[mode : mode + 1, :], 0.0), axis=1, keepdims=True)
        rates.append(jnp.broadcast_to(-rate, (slots, lanes)))
        coefs.append(jnp.broadcast_to(gain * jnp.sqrt(2.0 * rate), (slots, lanes)))
    lane_time = iota((slots, lanes), 1).astype(F32)

    def tap_step(chunk, carry):
        time = lane_time + (chunk * lanes).astype(F32)
        total = coefs[0] * jnp.exp(rates[0] * time)
        for mode in range(1, order):
            total = total + coefs[mode] * jnp.exp(rates[mode] * time)
        taps[pl.ds(pl.multiple_of(chunk * slots, slots), slots), :] = total
        return carry

    lax.fori_loop(0, n, tap_step, 0)

    for index in range(8, 14):
        loads[index].wait()

    def turned(real, imag, which):
        cos, sin = twi_ref[2 * which], twi_ref[2 * which + 1]
        return real * cos - imag * sin, real * sin + imag * cos

    def turned_back(real, imag, which):
        cos, sin = twi_ref[2 * which], twi_ref[2 * which + 1]
        return real * cos + imag * sin, imag * cos - real * sin

    half = iota((1, lanes), 1) < run

    def swapped(value):
        return pltpu.roll(value, run, axis=1)

    rows = []
    for i in range(slots):
        high, low = split(taps[pl.ds(i, n, stride=slots), :])
        mid = dot(cfw_ref[...], jnp.concatenate([high, high, low], axis=0))
        rows.append(jnp.concatenate(turned(mid[:n], mid[n:], 2), axis=1))
    high, low = split(jnp.concatenate(rows, axis=0))
    spec = dot(high, sec_ref[1]) + dot(low, sec_ref[1]) + dot(high, sec_ref[2])
    filt = jnp.concatenate([spec[:, :lanes], spec[:, lanes:]], axis=0)

    mine_all = jnp.floor(group_all * (1.0 / own)) == ctx.astype(F32)
    member = jnp.where(mine_all, 1.0, 0.0)
    before = jnp.where(row_i < col_i, 1.0, 0.0).astype(BF16)
    rank_all = dot(member.astype(BF16), before)
    for i in range(slots):
        hit = jnp.where(mine_all & (rank_all == float(i)), group_all, 0.0)
        gcol[pl.ds(i, n, stride=slots), :] = jnp.broadcast_to(
            jnp.sum(hit, axis=1, keepdims=True), (n, lanes)
        )
    first_own = (ctx * own).astype(F32)
    of_group = jnp.where(
        gcol[:chans, :] - first_own == iota((chans, lanes), 1).astype(F32), 1.0, 0.0
    )
    lagsel[...] = jnp.transpose(of_group)[: lagsel.shape[0], :].astype(BF16)

    await_all(p_recv, p_rsem)
    places = p_recv[...].reshape(n, lanes).astype(F32) * (1.0 / run)
    place = jnp.concatenate([places[:, 0:1], places[:, run : run + 1]], axis=0)
    place = jnp.concatenate([place, place + float(2 * n)], axis=0)
    onehot[...] = jnp.where(place == iota((4 * n, 4 * n), 1).astype(F32), 1.0, 0.0).astype(BF16)
    first = dot_nt(runt_ref[...], onehot[...]).astype(BF16)
    last = (dot(onehot[...], run_ref[...]) * (2.0 / (2 * lanes * n))).astype(BF16)
    last = jnp.concatenate([last[: 2 * n], last[2 * n :], last[: 2 * n]], axis=1)
    lane_i = iota((n, lanes), 1)
    left = lane_i < run

    await_all(x_recv, x_rsem)
    xs[: 2 * chans, :] = x_recv[...].astype(F32).reshape(2 * chans, lanes)
    gated_rows, weighted_rows = [[], []], [[], []]
    for i in range(slots):
        pair = []
        for row in (i, i + slots):
            value = xs[pl.ds(row, n, stride=2 * slots), :]
            both = jnp.concatenate(
                [jnp.where(left, value, 0.0), jnp.where(left, 0.0, value)], axis=0
            ).astype(BF16)
            pair.append(jnp.concatenate([both, both], axis=0))
        mid = dot(first, jnp.concatenate(pair, axis=1))
        for par in range(2):
            low_row = 2 * n * par
            for rows, off in ((gated_rows, 0), (weighted_rows, lanes)):
                piece = mid[low_row : low_row + 2 * n, off : off + lanes]
                rows[par].append(jnp.concatenate(turned(piece[:n], piece[n:], par), axis=1))

    def spectrum(rows):
        high, low = split(jnp.concatenate(rows[0] + rows[1], axis=0))
        both = dot(high, sec_ref[0])
        return both[:, :lanes] + both[:, lanes:] + dot(low, sec_ref[0, :, :lanes])

    gat = spectrum(gated_rows)
    wei = spectrum(weighted_rows)
    turned_gat = swapped(gat)
    gat_re = jnp.where(half, gat, turned_gat)
    gat_im = jnp.where(half, turned_gat, -gat)

    def channel(value, i):
        return value[i * n : (i + 1) * n]

    product = wei * gat_re + swapped(wei) * gat_im
    high, low = split(jnp.concatenate([product[:chans], product[chans:]], axis=1))
    mid = dot_nt(high, sec_ref[1]) + dot_nt(low, sec_ref[1]) + dot_nt(high, sec_ref[2])
    for i in range(slots):
        piece = channel(mid, i)
        high, low = split(
            jnp.concatenate(turned_back(piece[:, :lanes], piece[:, lanes:], 2), axis=0)
        )
        ys[pl.ds(i, n, stride=slots), :] = dot(
            cin_ref[...], jnp.concatenate([high, high, low], axis=0)
        )
    l_send[...] = ys[:chans, :].reshape(n, slots, lanes).astype(BF16)
    send_all(l_copy, ch, ch_steps)
    l_recv[ch] = l_send[moved(ch, flip, n)]

    high, low = split(filt * gat_re - swapped(filt) * gat_im)
    mid = dot_nt(jnp.concatenate([high, high], axis=1), sec_ref[0]) + dot_nt(
        low, sec_ref[0, :, :lanes]
    )
    for i in range(slots):
        stack = []
        for par in range(2):
            piece = channel(mid, par * slots + i)
            stack += list(turned_back(piece[:, :lanes], piece[:, lanes:], par))
        high, low = split(jnp.concatenate(stack, axis=0))
        value = dot(last, jnp.concatenate([high, high, low], axis=0))
        ys[pl.ds(i, n, stride=slots), :] = jnp.where(left, value[:n], value[n:])
    c_send[...] = ys[:chans, :].reshape(n, slots, lanes).astype(BF16)
    send_all(c_copy, ctx, ctx_steps)
    c_recv[ctx] = c_send[ctx]

    await_all(p_recv, p_ssem)
    await_all(x_send, x_ssem)
    await_all(l_recv, l_rsem)
    sums = dot(lagsel[...], l_recv[...].astype(F32).reshape(chans, lanes).astype(BF16))
    f_send[...] = sums[: f_send.shape[0]]
    far = pltpu.make_async_remote_copy(
        src_ref=f_send, dst_ref=f_recv, send_sem=f_sem.at[0], recv_sem=f_sem.at[1],
        device_id={"ctx": moved(ch, flip, n), "ch": ctx}, device_id_type=MESH,
    )
    far.start()

    await_all(l_send, l_ssem)
    await_all(c_recv, c_rsem)
    conv = dot(unsort[...], c_recv[...].astype(F32).reshape(chans, lanes).astype(BF16))
    out_ref[...] = (q_ref[...].astype(F32) * conv).astype(BF16)

    await_all(c_send, c_ssem)
    far.wait()
    fg_ref[...] = f_recv[...]


def put_kernel(out_ref, fg_ref, out_hbm, fg_hbm, sem):
    puts = [
        pltpu.make_async_copy(out_ref, out_hbm, sem.at[0]),
        pltpu.make_async_copy(fg_ref, fg_hbm, sem.at[1]),
    ]
    for put in puts:
        put.start()
    for put in puts:
        put.wait()


def shards(query_proj, key_proj, value_proj, cotangent, positions, group_of, decay_rates, residues):
    n = lax.axis_size("ctx")
    chans, lanes = query_proj.shape
    slots = chans // n
    groups_total, order = decay_rates.shape
    own = groups_total // lax.axis_size("ch")
    own_pad = -(-own // 16) * 16
    width = min(chans, lanes)
    tables = make_tables(n, lanes)
    args = (
        query_proj, key_proj, value_proj, cotangent,
        positions.reshape(1, lanes), group_of.reshape(-1, width),
        decay_rates.T, residues.T,
    ) + tuple(jnp.asarray(table) for table in tables)
    any_spec = pl.BlockSpec(memory_space=pl.ANY)
    vmem_spec = pl.BlockSpec(memory_space=pltpu.VMEM)
    dma = pltpu.SemaphoreType.DMA
    output, filter_grad = pl.pallas_call(
        functools.partial(kernel, n, slots, own, order),
        out_shape=(
            pltpu.VMEM((chans, lanes), BF16),
            pltpu.VMEM((own, lanes), F32),
        ),
        in_specs=[any_spec] * len(args),
        out_specs=(vmem_spec, vmem_spec),
        scratch_shapes=[
            pltpu.VMEM((arg.shape[0] + 8 * (at == 5),) + arg.shape[1:], arg.dtype)
            for at, arg in enumerate(args)
        ]
        + [
            pltpu.VMEM((n, 2 * slots, lanes), BF16),
            pltpu.VMEM((n, 2 * slots, lanes), BF16),
            pltpu.VMEM((n, 1, lanes), jnp.int32),
            pltpu.VMEM((n, slots, lanes), BF16),
            pltpu.VMEM((n, slots, lanes), BF16),
            pltpu.VMEM((n, slots, lanes), BF16),
            pltpu.VMEM((n, slots, lanes), BF16),
            pltpu.VMEM((own, lanes), F32),
            pltpu.VMEM((own, lanes), F32),
            pltpu.VMEM((2 * chans + 2 * slots, lanes), F32),
            pltpu.VMEM((chans + slots, lanes), F32),
            pltpu.VMEM((chans + slots, lanes), F32),
            pltpu.VMEM((chans + slots, lanes), F32),
            pltpu.VMEM((4 * n, 4 * n), BF16),
            pltpu.VMEM((chans, chans), BF16),
            pltpu.VMEM((own_pad, chans), BF16),
            dma((len(args),)),
            dma(()), dma(()), dma(()), dma(()),
            dma(()), dma(()), dma(()), dma(()),
            dma((2,)),
        ],
        compiler_params=pltpu.CompilerParams(collective_id=0, has_side_effects=True),
    )(*args)
    return pl.pallas_call(
        put_kernel,
        out_shape=(
            jax.ShapeDtypeStruct((chans, lanes), BF16),
            jax.ShapeDtypeStruct((own, lanes), F32),
        ),
        in_specs=[vmem_spec, vmem_spec],
        out_specs=(any_spec, any_spec),
        scratch_shapes=[dma((2,))],
    )(
        pltpu.with_memory_space_constraint(output, pltpu.VMEM),
        pltpu.with_memory_space_constraint(filter_grad, pltpu.VMEM),
    )


def solution(mesh):
    placed = (
        P("ch", "ctx"),
        P("ch", "ctx"),
        P("ch", "ctx"),
        P("ch", "ctx"),
        P("ctx"),
        P(),
        P(),
        P(),
    )
    return jax.shard_map(
        shards,
        mesh=mesh,
        in_specs=placed,
        out_specs=(P("ch", "ctx"), P("ch", "ctx")),
        check_vma=False,
    )
```

```python
import functools
import math

import jax
import jax.numpy as jnp
import ml_dtypes
import numpy as np
from jax import lax
from jax.experimental import pallas as pl
from jax.experimental.pallas import tpu as pltpu
from jax.sharding import PartitionSpec as P

MESH = pl.DeviceIdType.MESH
BF16 = jnp.bfloat16
F32 = jnp.float32


def halves(table):
    high = table.astype(ml_dtypes.bfloat16)
    low = (table - high.astype(np.float64)).astype(ml_dtypes.bfloat16)
    return high, low


def make_tables(n, lanes):
    run = lanes // 2
    extent = 2 * lanes * n
    turn = 2.0 * math.pi
    k = np.arange(n)
    j = np.arange(lanes) % run
    m = np.arange(run)

    def second(angle):
        cos, sin = np.cos(angle), np.sin(angle)
        return np.block([[cos, -sin], [sin, cos]])

    perm = second(turn * (j[:, None] * m[None, :] % run) / run)
    lane = np.arange(lanes)
    nat = [
        second(turn * (lane[:, None] * (2 * m + p)[None, :] % lanes) / lanes) for p in range(2)
    ]
    by_par = np.zeros((2, 2, run, 2, lanes))
    for p in range(2):
        by_par[:, p, :, p, :] = perm.reshape(2, 2, run, lanes)[:, 0]
    by_par = by_par.reshape(2 * lanes, 2 * lanes)
    second_tab = np.stack(
        [
            np.concatenate(halves(perm), axis=1),
            *halves(np.concatenate(nat, axis=1)),
            *halves(by_par),
        ]
    )

    twists = []
    for rows, cols in ((k, j), (k + 2 * n, j), (k, np.arange(lanes))):
        angle = turn * ((2 * rows[:, None] + 1) * cols[None, :] % (2 * extent)) / (2 * extent)
        twists += [np.cos(angle), -np.sin(angle)]
    twists += [np.concatenate([twists[i][:, :run], twists[i + 2][:, :run]], axis=1) for i in (0, 1)]
    twist_tab = np.stack(twists).astype(np.float32)

    kk = np.concatenate([k, k, k + 2 * n, k + 2 * n])
    part = np.concatenate([np.zeros(n), np.ones(n)] * 2)
    angle = turn * ((2 * kk[None, :] + 1) * np.arange(2 * n)[:, None] % (8 * n)) / (8 * n)
    first = np.where(part[None, :] == 0, np.cos(angle), -np.sin(angle))
    run_tab = np.concatenate(halves(first), axis=0)

    kn = np.concatenate([k, k])
    partn = np.concatenate([np.zeros(n), np.ones(n)])
    angle = turn * ((2 * kn[:, None] + 1) * k[None, :] % (4 * n)) / (4 * n)
    chunk = np.where(partn[:, None] == 0, np.cos(angle), -np.sin(angle))
    high, low = halves(chunk)
    chunk_fwd = np.concatenate([high, low, high], axis=1)
    scale = 2.0 / extent
    high, low = halves(chunk.T * scale)
    chunk_inv = np.concatenate([high, low, high], axis=1)
    return second_tab, twist_tab, run_tab, np.ascontiguousarray(run_tab.T), chunk_fwd, chunk_inv


def dot(left, right):
    return lax.dot_general(left, right, (((1,), (0,)), ((), ())), preferred_element_type=F32)


def dot_nt(left, right):
    return lax.dot_general(left, right, (((1,), (1,)), ((), ())), preferred_element_type=F32)


def split(value):
    high = value.astype(BF16)
    return high, (value - high.astype(F32)).astype(BF16)


def partners(n, unit):
    ring = n // 2
    steps = [(half, low) for half in range(2) for low in range(ring) if half or low]
    return sorted(steps, key=lambda s: -(min(s[1], ring - s[1]) / unit + (3 - unit) * s[0]))


def moved(index, step, n):
    ring = n // 2
    return ((index + step[0] * ring) & ring) + ((index + step[1]) & (ring - 1))


def iota(shape, axis):
    return lax.broadcasted_iota(jnp.int32, shape, axis)


def kernel(
    n,
    slots,
    own,
    order,
    q_hbm, k_hbm, v_hbm, c_hbm, pos_hbm, grp_hbm, dec_hbm, res_hbm,
    sec_hbm, twi_hbm, run_hbm, runt_hbm, cfw_hbm, cin_hbm,
    out_ref, fg_ref,
    q_ref, k_ref, v_ref, c_ref, pos_ref, grp_ref, dec_ref, res_ref,
    sec_ref, twi_ref, run_ref, runt_ref, cfw_ref, cin_ref,
    x_send, x_recv, p_recv, c_send, c_recv, l_send, l_recv, f_send, f_recv,
    xs, taps, gcol, ys, onehot, unsort, lagsel,
    in_sem, x_ssem, x_rsem, p_ssem, p_rsem, c_ssem, c_rsem, l_ssem, l_rsem, f_sem,
):
    lanes = 128
    run = lanes // 2
    chans = n * slots
    ctx = lax.axis_index("ctx")
    ch = lax.axis_index("ch")

    sources = (grp_hbm, k_hbm, v_hbm, c_hbm, q_hbm, pos_hbm, dec_hbm, res_hbm,
               runt_hbm, run_hbm, cfw_hbm, twi_hbm, sec_hbm, cin_hbm)
    targets = (grp_ref.at[pl.ds(0, grp_hbm.shape[0])], k_ref, v_ref, c_ref, q_ref, pos_ref, dec_ref, res_ref,
               runt_ref, run_ref, cfw_ref, twi_ref, sec_ref, cin_ref)
    loads = [
        pltpu.make_async_copy(source, target, in_sem.at[index])
        for index, (source, target) in enumerate(zip(sources, targets))
    ]
    ctx_steps = partners(n, 1)
    ch_steps = partners(n, 2)
    barrier = pltpu.get_barrier_semaphore()
    for step in ctx_steps:
        pl.semaphore_signal(
            barrier, inc=1, device_id={"ctx": moved(ctx, step, n)}, device_id_type=MESH
        )
    for load in loads:
        load.start()
    for step in ch_steps:
        pl.semaphore_signal(
            barrier, inc=1, device_id={"ch": moved(ch, step, n)}, device_id_type=MESH
        )

    loads[0].wait()
    if chans > lanes:
        per_row = chans // lanes
        pieces = [grp_ref[pl.ds(i, n, stride=per_row), :] for i in range(per_row)]
        group_all = jnp.concatenate(pieces, axis=1).astype(F32)
        pieces = [grp_ref[pl.ds(ch * per_row + i, 1), :] for i in range(per_row)]
        group_row = jnp.concatenate(pieces, axis=1).astype(F32)
    else:
        group_all = grp_ref[:n, :].astype(F32)
        group_row = grp_ref[pl.ds(ch, 1), :].astype(F32)
    owner_row = jnp.floor(group_row * (1.0 / own))
    owner_rows = jnp.broadcast_to(owner_row, (chans, chans))
    owner_cols = jnp.transpose(owner_rows)
    row_i = iota((chans, chans), 0)
    col_i = iota((chans, chans), 1)
    same = owner_rows == owner_cols
    rank_row = jnp.sum(jnp.where(same & (row_i < col_i), 1.0, 0.0), axis=0, keepdims=True)
    rank_col = jnp.sum(jnp.where(same & (col_i < row_i), 1.0, 0.0), axis=1, keepdims=True)
    slot_row = owner_row * slots + rank_row
    slot_col = owner_cols[:, 0:1] * slots + rank_col
    sort = jnp.where(slot_row == row_i.astype(F32), 1.0, 0.0).astype(BF16)
    unsort[...] = jnp.where(slot_col == col_i.astype(F32), 1.0, 0.0).astype(BF16)

    for index in range(1, 5):
        loads[index].wait()
    gated = (k_ref[...].astype(F32) * v_ref[...].astype(F32)).astype(BF16)
    weighted = (c_ref[...].astype(F32) * q_ref[...].astype(F32)).astype(BF16)
    gated = dot(sort, gated).reshape(n, slots, lanes)
    weighted = dot(sort, weighted).reshape(n, slots, lanes)
    x_send[...] = jnp.concatenate([gated, weighted], axis=1).astype(BF16)
    loads[5].wait()

    pl.semaphore_wait(barrier, 2 * (n - 1))

    def pos_copy(target):
        return pltpu.make_async_remote_copy(
            src_ref=pos_ref, dst_ref=p_recv.at[ctx], send_sem=p_ssem, recv_sem=p_rsem,
            device_id={"ctx": target}, device_id_type=MESH,
        )

    def x_copy(target):
        return pltpu.make_async_remote_copy(
            src_ref=x_send.at[target], dst_ref=x_recv.at[ctx], send_sem=x_ssem, recv_sem=x_rsem,
            device_id={"ctx": target}, device_id_type=MESH,
        )

    def c_copy(target):
        return pltpu.make_async_remote_copy(
            src_ref=c_send.at[target], dst_ref=c_recv.at[ctx], send_sem=c_ssem, recv_sem=c_rsem,
            device_id={"ctx": target}, device_id_type=MESH,
        )

    flip = (1, n // 4)

    def l_copy(target):
        return pltpu.make_async_remote_copy(
            src_ref=l_send.at[moved(target, flip, n)], dst_ref=l_recv.at[ch],
            send_sem=l_ssem, recv_sem=l_rsem,
            device_id={"ch": target}, device_id_type=MESH,
        )

    def send_all(copy, me, steps):
        for step in steps:
            copy(moved(me, step, n)).start()

    def await_all(ref, sem):
        part = ref.at[pl.ds(0, n - 1)]
        pltpu.make_async_copy(part, part, sem).wait()

    for step in ctx_steps:
        pos_copy(moved(ctx, step, n)).start()
        x_copy(moved(ctx, step, n)).start()
    x_recv[ctx] = x_send[ctx]
    p_recv[ctx] = pos_ref[...]

    loads[6].wait()
    loads[7].wait()
    me_slot = iota((slots, chans), 0).astype(F32) + (ctx * slots).astype(F32)
    mine = jnp.where(slot_row == me_slot, group_row, 0.0)
    my_group = jnp.sum(mine, axis=1, keepdims=True)
    groups_total = dec_ref.shape[1]
    pick = my_group == iota((slots, groups_total), 1).astype(F32)
    rates, coefs = [], []
    for mode in range(order):
        rate = jnp.sum(jnp.where(pick, dec_ref[mode : mode + 1, :], 0.0), axis=1, keepdims=True)
        gain = jnp.sum(jnp.where(pick, res_ref[mode : mode + 1, :], 0.0), axis=1, keepdims=True)
        rates.append(jnp.broadcast_to(-rate, (slots, lanes)))
        coefs.append(jnp.broadcast_to(gain * jnp.sqrt(2.0 * rate), (slots, lanes)))
    lane_time = iota((slots, lanes), 1).astype(F32)

    def tap_step(chunk, carry):
        time = lane_time + (chunk * lanes).astype(F32)
        total = coefs[0] * jnp.exp(rates[0] * time)
        for mode in range(1, order):
            total = total + coefs[mode] * jnp.exp(rates[mode] * time)
        taps[pl.ds(pl.multiple_of(chunk * slots, slots), slots), :] = total
        return carry

    lax.fori_loop(0, n, tap_step, 0)

    for index in range(8, 14):
        loads[index].wait()

    def turned(real, imag, which):
        cos, sin = twi_ref[2 * which], twi_ref[2 * which + 1]
        return real * cos - imag * sin, real * sin + imag * cos

    def turned_back(real, imag, which):
        cos, sin = twi_ref[2 * which], twi_ref[2 * which + 1]
        return real * cos + imag * sin, imag * cos - real * sin

    half = iota((1, lanes), 1) < run

    def swapped(value):
        return pltpu.roll(value, run, axis=1)

    rows = []
    for i in range(slots):
        high, low = split(taps[pl.ds(i, n, stride=slots), :])
        mid = dot(cfw_ref[...], jnp.concatenate([high, high, low], axis=0))
        rows.append(jnp.concatenate(turned(mid[:n], mid[n:], 2), axis=1))
    high, low = split(jnp.concatenate(rows, axis=0))
    spec = dot(high, sec_ref[1]) + dot(low, sec_ref[1]) + dot(high, sec_ref[2])
    filt = jnp.concatenate([spec[:, :lanes], spec[:, lanes:]], axis=0)

    mine_all = jnp.floor(group_all * (1.0 / own)) == ctx.astype(F32)
    member = jnp.where(mine_all, 1.0, 0.0)
    before = jnp.where(row_i < col_i, 1.0, 0.0).astype(BF16)
    rank_all = dot(member.astype(BF16), before)
    for i in range(slots):
        hit = jnp.where(mine_all & (rank_all == float(i)), group_all, 0.0)
        gcol[pl.ds(i, n, stride=slots), :] = jnp.broadcast_to(
            jnp.sum(hit, axis=1, keepdims=True), (n, lanes)
        )
    first_own = (ctx * own).astype(F32)
    of_group = jnp.where(
        gcol[:chans, :] - first_own == iota((chans, lanes), 1).astype(F32), 1.0, 0.0
    )
    lagsel[...] = jnp.transpose(of_group)[: lagsel.shape[0], :].astype(BF16)

    await_all(p_recv, p_rsem)
    places = p_recv[...].reshape(n, lanes).astype(F32) * (1.0 / run)
    place = jnp.concatenate([places[:, 0:1], places[:, run : run + 1]], axis=0)
    place = jnp.concatenate([place, place + float(2 * n)], axis=0)
    onehot[...] = jnp.where(place == iota((4 * n, 4 * n), 1).astype(F32), 1.0, 0.0).astype(BF16)
    first = dot_nt(runt_ref[...], onehot[...]).astype(BF16)
    last = (dot(onehot[...], run_ref[...]) * (2.0 / (2 * lanes * n))).astype(BF16)
    last = jnp.concatenate([last[: 2 * n], last[2 * n :], last[: 2 * n]], axis=1)
    lane_i = iota((n, lanes), 1)
    left = lane_i < run

    await_all(x_recv, x_rsem)
    xs[: 2 * chans, :] = x_recv[...].astype(F32).reshape(2 * chans, lanes)
    gated_rows, weighted_rows = [], []
    for i in range(slots):
        pair = []
        for row in (i, i + slots):
            value = xs[pl.ds(row, n, stride=2 * slots), :]
            both = jnp.concatenate(
                [jnp.where(left, value, 0.0), jnp.where(left, 0.0, value)], axis=0
            ).astype(BF16)
            pair.append(jnp.concatenate([both, both], axis=0))
        mid = dot(first, jnp.concatenate(pair, axis=1))
        for rows, off in ((gated_rows, 0), (weighted_rows, lanes)):
            even, odd = mid[: 2 * n, off : off + lanes], mid[2 * n :, off : off + lanes]
            piece = jnp.where(half, even, odd) + swapped(jnp.where(half, odd, even))
            rows.append(jnp.concatenate(turned(piece[:n], piece[n:], 3), axis=1))

    def spectrum(rows):
        high, low = split(jnp.concatenate(rows, axis=0))
        spec = dot(high, sec_ref[3]) + dot(low, sec_ref[3]) + dot(high, sec_ref[4])
        return jnp.concatenate([spec[:, :lanes], spec[:, lanes:]], axis=0)

    gat = spectrum(gated_rows)
    wei = spectrum(weighted_rows)
    turned_gat = swapped(gat)
    gat_re = jnp.where(half, gat, turned_gat)
    gat_im = jnp.where(half, turned_gat, -gat)

    def channel(value, i):
        return value[i * n : (i + 1) * n]

    product = wei * gat_re + swapped(wei) * gat_im
    high, low = split(jnp.concatenate([product[:chans], product[chans:]], axis=1))
    mid = dot_nt(high, sec_ref[1]) + dot_nt(low, sec_ref[1]) + dot_nt(high, sec_ref[2])
    for i in range(slots):
        piece = channel(mid, i)
        high, low = split(
            jnp.concatenate(turned_back(piece[:, :lanes], piece[:, lanes:], 2), axis=0)
        )
        ys[pl.ds(i, n, stride=slots), :] = dot(
            cin_ref[...], jnp.concatenate([high, high, low], axis=0)
        )
    l_send[...] = ys[:chans, :].reshape(n, slots, lanes).astype(BF16)
    send_all(l_copy, ch, ch_steps)
    l_recv[ch] = l_send[moved(ch, flip, n)]

    high, low = split(filt * gat_re - swapped(filt) * gat_im)
    mid = dot_nt(jnp.concatenate([high, high], axis=1), sec_ref[0]) + dot_nt(
        low, sec_ref[0, :, :lanes]
    )
    for i in range(slots):
        stack = []
        for par in range(2):
            piece = channel(mid, par * slots + i)
            stack += list(turned_back(piece[:, :lanes], piece[:, lanes:], par))
        high, low = split(jnp.concatenate(stack, axis=0))
        value = dot(last, jnp.concatenate([high, high, low], axis=0))
        ys[pl.ds(i, n, stride=slots), :] = jnp.where(left, value[:n], value[n:])
    c_send[...] = ys[:chans, :].reshape(n, slots, lanes).astype(BF16)
    send_all(c_copy, ctx, ctx_steps)
    c_recv[ctx] = c_send[ctx]

    await_all(p_recv, p_ssem)
    await_all(x_send, x_ssem)
    await_all(l_recv, l_rsem)
    sums = dot(lagsel[...], l_recv[...].astype(F32).reshape(chans, lanes).astype(BF16))
    f_send[...] = sums[: f_send.shape[0]]
    far = pltpu.make_async_remote_copy(
        src_ref=f_send, dst_ref=f_recv, send_sem=f_sem.at[0], recv_sem=f_sem.at[1],
        device_id={"ctx": moved(ch, flip, n), "ch": ctx}, device_id_type=MESH,
    )
    far.start()

    await_all(l_send, l_ssem)
    await_all(c_recv, c_rsem)
    conv = dot(unsort[...], c_recv[...].astype(F32).reshape(chans, lanes).astype(BF16))
    out_ref[...] = (q_ref[...].astype(F32) * conv).astype(BF16)

    await_all(c_send, c_ssem)
    far.wait()
    fg_ref[...] = f_recv[...]


def put_kernel(out_ref, fg_ref, out_hbm, fg_hbm, sem):
    puts = [
        pltpu.make_async_copy(out_ref, out_hbm, sem.at[0]),
        pltpu.make_async_copy(fg_ref, fg_hbm, sem.at[1]),
    ]
    for put in puts:
        put.start()
    for put in puts:
        put.wait()


def shards(query_proj, key_proj, value_proj, cotangent, positions, group_of, decay_rates, residues):
    n = lax.axis_size("ctx")
    chans, lanes = query_proj.shape
    slots = chans // n
    groups_total, order = decay_rates.shape
    own = groups_total // lax.axis_size("ch")
    own_pad = -(-own // 16) * 16
    width = min(chans, lanes)
    tables = make_tables(n, lanes)
    args = (
        query_proj, key_proj, value_proj, cotangent,
        positions.reshape(1, lanes), group_of.reshape(-1, width),
        decay_rates.T, residues.T,
    ) + tuple(jnp.asarray(table) for table in tables)
    any_spec = pl.BlockSpec(memory_space=pl.ANY)
    vmem_spec = pl.BlockSpec(memory_space=pltpu.VMEM)
    dma = pltpu.SemaphoreType.DMA
    output, filter_grad = pl.pallas_call(
        functools.partial(kernel, n, slots, own, order),
        out_shape=(
            pltpu.VMEM((chans, lanes), BF16),
            pltpu.VMEM((own, lanes), F32),
        ),
        in_specs=[any_spec] * len(args),
        out_specs=(vmem_spec, vmem_spec),
        scratch_shapes=[
            pltpu.VMEM((arg.shape[0] + 8 * (at == 5),) + arg.shape[1:], arg.dtype)
            for at, arg in enumerate(args)
        ]
        + [
            pltpu.VMEM((n, 2 * slots, lanes), BF16),
            pltpu.VMEM((n, 2 * slots, lanes), BF16),
            pltpu.VMEM((n, 1, lanes), jnp.int32),
            pltpu.VMEM((n, slots, lanes), BF16),
            pltpu.VMEM((n, slots, lanes), BF16),
            pltpu.VMEM((n, slots, lanes), BF16),
            pltpu.VMEM((n, slots, lanes), BF16),
            pltpu.VMEM((own, lanes), F32),
            pltpu.VMEM((own, lanes), F32),
            pltpu.VMEM((2 * chans + 2 * slots, lanes), F32),
            pltpu.VMEM((chans + slots, lanes), F32),
            pltpu.VMEM((chans + slots, lanes), F32),
            pltpu.VMEM((chans + slots, lanes), F32),
            pltpu.VMEM((4 * n, 4 * n), BF16),
            pltpu.VMEM((chans, chans), BF16),
            pltpu.VMEM((own_pad, chans), BF16),
            dma((len(args),)),
            dma(()), dma(()), dma(()), dma(()),
            dma(()), dma(()), dma(()), dma(()),
            dma((2,)),
        ],
        compiler_params=pltpu.CompilerParams(collective_id=0, has_side_effects=True),
    )(*args)
    return pl.pallas_call(
        put_kernel,
        out_shape=(
            jax.ShapeDtypeStruct((chans, lanes), BF16),
            jax.ShapeDtypeStruct((own, lanes), F32),
        ),
        in_specs=[vmem_spec, vmem_spec],
        out_specs=(any_spec, any_spec),
        scratch_shapes=[dma((2,))],
    )(
        pltpu.with_memory_space_constraint(output, pltpu.VMEM),
        pltpu.with_memory_space_constraint(filter_grad, pltpu.VMEM),
    )


def solution(mesh):
    placed = (
        P("ch", "ctx"),
        P("ch", "ctx"),
        P("ch", "ctx"),
        P("ch", "ctx"),
        P("ctx"),
        P(),
        P(),
        P(),
    )
    return jax.shard_map(
        shards,
        mesh=mesh,
        in_specs=placed,
        out_specs=(P("ch", "ctx"), P("ch", "ctx")),
        check_vma=False,
    )
```
